256 devices in a mesh: seq: 64 (over z, y, core), tp: 4 (over x).
Axes of the slice: x: 4, y: 4, z: 8, core: 2. Of those that a mesh axis runs over, the one named last changes fastest.
Arguments:
- normed: bfloat16 [32768, 2048], P('seq', 'tp'), may hold values from -24 to 24
- cluster: int32 [32768, 1], P('seq'), may hold values from 0 to 127; in each aligned block of 512 rows (0 to 511, 512 to 1023, ...) at most 8 rows name the same one
- w_query: bfloat16 [2048, 2048], P(None, 'tp'), may hold values from -1 to 1
- w_key: bfloat16 [2048, 2048], P(None, 'tp'), may hold values from -1 to 1
- w_value: bfloat16 [2048, 2048], P(None, 'tp'), may hold values from -0.125 to 0.125
- w_out: bfloat16 [2048, 2048], P('tp'), may hold values from -0.125 to 0.125
- grad_out: bfloat16 [32768, 2048], P('seq', 'tp'), may hold values from -6 to 6
Outputs:
- attended: bfloat16 [32768, 2048], P('seq', 'tp')
- grad_normed: float32 [32768, 2048], P('seq', 'tp')
The draws below stay inside these ranges and needn't reach their ends.
Inputs may be any that keep to these rules, and one draw needn't show every extreme that they name: Among the tokens of one index of seq no cluster id appears more than 8 times, and some id appears exactly 8 times; every id appears somewhere.
All inputs are finite; a program needn't handle non-finite values.
Results may differ from the reference program's by a relative error of at most 0.011.
The reference program's roundings to bfloat16 on the way count: a program that leaves them out, or rounds other values in their place, can miss the bound.
Values may be sent and summed in bfloat16 or wider, within the bound.
A program may use at most 128 MiB of HBM per device.

```python
import math
import jax
import jax.numpy as jnp
import numpy as np
from jax import lax

D = 2048
HEADS = 16
HEAD_DIM = 128
CLUSTERS = 128
CAP = 256
TOK_DEV = 512
TOKENS = 32768
MOST = 8


def weight_pair(key):
    first = jax.random.normal(jax.random.fold_in(key, 11), (D, D), jnp.float32)
    second = jax.random.normal(jax.random.fold_in(key, 12), (D, D), jnp.float32)
    first = jnp.clip(first, -5.5, 5.5) / math.sqrt(D)
    second = jnp.clip(second, -5.5, 5.5) / math.sqrt(D)
    return (first, second)


def draw_w_query(key, part):
    first, second = weight_pair(key)
    return first.astype(jnp.bfloat16)


def draw_w_key(key, part):
    first, second = weight_pair(key)
    return second.astype(jnp.bfloat16)


def draw_normed(key, part):
    values = jax.random.normal(jax.random.fold_in(key, 24), (TOKENS, D), jnp.float32)
    return jnp.clip(values, -6.0, 6.0).astype(jnp.bfloat16)


def level_of(stream_key, shape, shards, least, high):
    def one(dim, shards_of):
        draws = jax.random.uniform(jax.random.fold_in(jax.random.fold_in(stream_key, 6), dim), (shards_of,), jnp.float32, least / len(shards), high / len(shards))
        return jnp.repeat(jnp.exp(draws), shape[dim] // shards_of).reshape((-1,) + (1,) * (len(shape) - dim - 1))

    gain = one(*shards[0])
    for cut in shards[1:]:
        gain = gain * one(*cut)
    return gain


def shared_out(own_key, own, number, rows, count, top, bound, skew):
    sequence = jax.random.permutation(own_key, count)
    crowded, usual = portions_of(count, rows * top, bound, skew, True), portions_of(count, rows * top, bound, skew, False)
    places = jnp.arange(count)

    def named(sizes, offset_by):
        used = int((sizes > 0).sum())
        fixed = max(1, used // 4)
        moved = fixed + (places - fixed + offset_by * (used - fixed)) % max(1, count - fixed)
        return jnp.zeros((count,), jnp.int32).at[sequence[jnp.where(places < fixed, places, moved)]].set(jnp.asarray(sizes, jnp.int32))

    sizes = jnp.where(number % 4 == 0, named(crowded, number // 4), named(usual, number - number // 4 - 1))
    mixed = jax.random.permutation(jax.random.fold_in(own, 3), count)
    donor, receiver = mixed[0:count // 2 * 2:2], mixed[1:count // 2 * 2:2]
    slack = jnp.minimum(sizes[donor] - 1, bound - sizes[receiver]) // 2
    slack = jnp.where((donor == sequence[0]) | (receiver == sequence[0]) | (sizes[receiver] == 0), 0, jnp.maximum(slack, 0))
    moved = jax.random.randint(jax.random.fold_in(own, 4), (count // 2,), 0, 1 << 20) % (slack + 1)
    sizes = sizes.at[donor].add(-moved).at[receiver].add(moved)
    items = jnp.searchsorted(jnp.cumsum(sizes), jnp.arange(rows * top), side="right").astype(jnp.int32)
    listing = items.reshape(top, rows).T
    listing = listing[jax.random.permutation(jax.random.fold_in(own, 1), rows)]
    offset_by = jax.random.randint(jax.random.fold_in(own, 2), (rows, 1), 0, top)
    return jnp.take_along_axis(listing, (jnp.arange(top)[None, :] + offset_by) % top, axis=1)


def portions_of(number_of, total, limit, slope, full):
    weights = [(1 << 20) // math.isqrt(rank ** slope) + 1 for rank in range(1, number_of + 1)]
    largest = limit if full else min(limit, max(-(-total // number_of), total * weights[0] // sum(weights)))
    least = 1 if total - largest >= number_of - 1 else 0
    given, surplus = [largest] + [least] * (number_of - 1), total - largest - least * (number_of - 1)
    while surplus > 0:
        free = [i for i in range(1, number_of) if given[i] < largest] or [i for i in range(1, number_of) if given[i] < limit]
        whole, left = sum([weights[i] for i in free]), surplus
        for i in free:
            extra = min(limit - given[i], max(1, left * weights[i] // whole), surplus)
            given[i] = given[i] + extra
            surplus = surplus - extra
    return np.array(given)


def gaussian(key, extent, width, most, pieces=(), kind=jnp.bfloat16):
    result = jax.random.normal(key, extent, jnp.float32) * width
    if len(pieces) > 0:
        result = level_of(key, extent, pieces, -0.22, 0.18) * result
    return jnp.clip(result, min=-most, max=most).astype(kind)


def setup_inputs(seed: int = 0) -> dict:
    streams_of = jax.random.split(jax.random.key(seed), 8)
    normed = draw_normed(jax.random.fold_in(streams_of[7], 71), 0)
    cluster_keys = jax.random.split(jax.random.fold_in(streams_of[1], 1), TOKENS // TOK_DEV)
    cluster_turns = jax.random.permutation(jax.random.fold_in(streams_of[1], 3), TOKENS // TOK_DEV)
    cluster = jax.vmap(lambda own, number: shared_out(jax.random.fold_in(streams_of[1], 2), own, number, TOK_DEV, CLUSTERS, 1, MOST, 2))(cluster_keys, cluster_turns).reshape((TOKENS, 1))
    w_query = draw_w_query(jax.random.fold_in(streams_of[7], 71), 0)
    w_key = draw_w_key(jax.random.fold_in(streams_of[7], 71), 0)
    w_value = gaussian(streams_of[4], (D, D), D ** -0.5, 0.125, ((1, 4),))
    w_out = gaussian(streams_of[5], (D, D), D ** -0.5, 0.125, ((0, 4),))
    grad_out = gaussian(streams_of[6], (TOKENS, D), 1.0, 6.0, ((0, 64), (1, 4)))
    return {"normed": normed, "cluster": cluster, "w_query": w_query, "w_key": w_key, "w_value": w_value, "w_out": w_out, "grad_out": grad_out}


def reference(normed, cluster, w_query, w_key, w_value, w_out, grad_out):
    cluster_ids = cluster[:, 0].astype(jnp.int32)
    columns = jnp.arange(CLUSTERS, dtype=jnp.int32)
    one_hot = (cluster_ids[:, None] == columns[None, :]).astype(jnp.int32)
    running = jnp.cumsum(one_hot, axis=0)
    place_rank = jnp.sum((running - one_hot) * one_hot, axis=1).astype(jnp.int32)
    kept = place_rank < CAP
    kept_rows = kept.astype(jnp.bfloat16)[:, None]
    queries = lax.optimization_barrier(jnp.dot(normed, w_query, preferred_element_type=jnp.float32).astype(jnp.bfloat16))
    keys_proj = lax.optimization_barrier(jnp.dot(normed, w_key, preferred_element_type=jnp.float32).astype(jnp.bfloat16))
    values_proj = lax.optimization_barrier(jnp.dot(normed, w_value, preferred_element_type=jnp.float32).astype(jnp.bfloat16))
    head_grads = lax.optimization_barrier(jnp.dot(grad_out, w_out.T, preferred_element_type=jnp.float32).astype(jnp.bfloat16) * kept_rows)
    slot_index = jnp.where(kept, cluster_ids * CAP + place_rank, CLUSTERS * CAP).astype(jnp.int32)
    filler = jnp.full((CLUSTERS * CAP + 1,), TOKENS, jnp.int32)
    token_of_slot = filler.at[slot_index].set(jnp.arange(TOKENS, dtype=jnp.int32))[: CLUSTERS * CAP].reshape(CLUSTERS, CAP)
    score_scale = HEAD_DIM ** -0.5

    def per_cluster(members):
        usable = members < TOKENS

        def pick(source):
            taken = jnp.take(source, members, axis=0, mode="fill", fill_value=0)
            return taken.reshape(CAP, HEADS, HEAD_DIM).astype(jnp.float32)

        query = pick(queries)
        key_rows = pick(keys_proj)
        value_rows = pick(values_proj)
        grad_rows = pick(head_grads)
        scores = jnp.einsum("qhd,khd->hqk", query, key_rows) * score_scale
        scores = jnp.where(usable[None, None, :], scores, -1e30)
        row_top = jnp.max(scores, axis=-1, keepdims=True)
        raised = jnp.exp(scores - row_top)
        probs = raised / jnp.sum(raised, axis=-1, keepdims=True)
        rounded = lax.optimization_barrier(probs.astype(jnp.bfloat16)).astype(jnp.float32)
        mixed = jnp.einsum("hqk,khd->qhd", rounded, value_rows).astype(jnp.bfloat16)
        grad_value = jnp.einsum("hqk,qhd->khd", rounded, grad_rows).astype(jnp.bfloat16)
        grad_probs = jnp.einsum("qhd,khd->hqk", grad_rows, value_rows)
        inner = jnp.sum(grad_probs * probs, axis=-1, keepdims=True)
        grad_scores = (probs * (grad_probs - inner) * score_scale).astype(jnp.bfloat16)
        grad_scores = lax.optimization_barrier(grad_scores).astype(jnp.float32)
        grad_query = jnp.einsum("hqk,khd->qhd", grad_scores, key_rows).astype(jnp.bfloat16)
        grad_key = jnp.einsum("hqk,qhd->khd", grad_scores, query).astype(jnp.bfloat16)
        return (mixed.reshape(CAP, D), grad_query.reshape(CAP, D), grad_key.reshape(CAP, D), grad_value.reshape(CAP, D))

    mixed_slots, query_slots, key_slots, value_slots = lax.map(per_cluster, token_of_slot)
    flat = token_of_slot.reshape(-1)

    def scatter_back(values):
        return jnp.zeros((TOKENS, D), jnp.bfloat16).at[flat].set(values.reshape(-1, D), mode="drop")

    mixed_heads = scatter_back(mixed_slots)
    attended = jnp.dot(mixed_heads, w_out, preferred_element_type=jnp.float32).astype(jnp.bfloat16)
    grad_normed = jnp.dot(scatter_back(query_slots), w_query.T, preferred_element_type=jnp.float32)
    grad_normed = grad_normed + jnp.dot(scatter_back(key_slots), w_key.T, preferred_element_type=jnp.float32)
    grad_normed = grad_normed + jnp.dot(scatter_back(value_slots), w_value.T, preferred_element_type=jnp.float32)
    return (attended, grad_normed)
```

```python
import jax
import jax.numpy as jnp
from jax import lax
from jax.sharding import PartitionSpec as P

HEAD_DIM = 128
CLUSTERS = 128
CAP = 256
MOST = 8
EMPTY = 128.0


def attention(query, key_rows, value_rows, grad_rows, usable):
    groups, rows, width = query.shape
    scale = HEAD_DIM ** (-0.5)

    def heads(x):
        return x.reshape(groups, rows, width // HEAD_DIM, HEAD_DIM)

    def product(spec, a, b):
        return jnp.einsum(spec, a, b, preferred_element_type=jnp.float32)

    query, key_rows, value_rows, grad_rows = (
        heads(query),
        heads(key_rows),
        heads(value_rows),
        heads(grad_rows),
    )
    scores = product("cqhd,ckhd->chqk", query, key_rows) * scale
    scores = jnp.where(usable[:, None, None, :], scores, -1e30)
    raised = jnp.exp(scores - jnp.max(scores, axis=-1, keepdims=True))
    probs = raised / jnp.sum(raised, axis=-1, keepdims=True)
    rounded = probs.astype(jnp.bfloat16)
    mixed = product("chqk,ckhd->cqhd", rounded, value_rows)
    grad_value = product("chqk,cqhd->ckhd", rounded, grad_rows)
    grad_probs = product("cqhd,ckhd->chqk", grad_rows, value_rows)
    inner = jnp.sum(grad_probs * probs, axis=-1, keepdims=True)
    grad_scores = (probs * (grad_probs - inner) * scale).astype(jnp.bfloat16)
    grad_query = product("chqk,ckhd->cqhd", grad_scores, key_rows)
    grad_key = product("chqk,cqhd->ckhd", grad_scores, query)

    def flat(x):
        return x.astype(jnp.bfloat16).reshape(groups * rows, width)

    return flat(mixed), flat(grad_query), flat(grad_key), flat(grad_value)


def body(normed, cluster, w_query, w_key, w_value, w_out, grad_out):
    seq_count = lax.axis_size("seq")
    tp_count = lax.axis_size("tp")
    here = CLUSTERS // seq_count
    tokens, width = normed.shape
    ids = cluster[:, 0]
    order = jnp.arange(tokens, dtype=jnp.int32)
    same = (ids[:, None] == ids[None, :]) & (order[None, :] < order[:, None])
    rank = jnp.sum(same.astype(jnp.int32), axis=1)
    slot = ids * MOST + rank
    places = jnp.arange(CLUSTERS * MOST, dtype=jnp.int32)
    spread = (places[:, None] == slot[None, :]).astype(jnp.bfloat16)
    both = jnp.concatenate([normed, grad_out], axis=1)
    packed = jnp.dot(spread, both, preferred_element_type=jnp.float32)
    filled = jnp.sum(spread.astype(jnp.float32), axis=1, keepdims=True)
    first = (jnp.arange(2 * width) == 0).astype(jnp.float32)
    packed = (packed + (1.0 - filled) * first[None, :] * EMPTY).astype(jnp.bfloat16)
    packed = packed.reshape(seq_count, here, MOST, 2 * width)
    arrived = lax.all_to_all(packed, "seq", split_axis=0, concat_axis=0, tiled=True)
    arrived = jnp.swapaxes(arrived, 0, 1).reshape(here, seq_count * MOST, 2 * width)
    valid = arrived[:, :, 0].astype(jnp.float32) < 0.5 * EMPTY
    slots = seq_count * MOST
    index = jnp.arange(slots)
    before = (index[:, None] < index[None, :]).astype(jnp.bfloat16)
    place = jnp.dot(valid.astype(jnp.bfloat16), before, preferred_element_type=jnp.float32)
    rows = jnp.arange(CAP, dtype=jnp.float32)
    choose = (
        (place[:, None, :] == rows[None, :, None]) & valid[:, None, :]
    ).astype(jnp.bfloat16)
    usable = jnp.sum(choose.astype(jnp.float32), axis=2) > 0.5
    compact = jnp.einsum(
        "crs,csf->crf", choose, arrived, preferred_element_type=jnp.float32
    ).astype(jnp.bfloat16)
    compact = compact.reshape(here * CAP, 2 * width)
    gathered = lax.all_gather(compact, "tp", axis=0)
    x = jnp.swapaxes(gathered[:, :, :width], 0, 1).reshape(here * CAP, tp_count * width)
    dy = jnp.swapaxes(gathered[:, :, width:], 0, 1).reshape(here * CAP, tp_count * width)

    def project(w):
        y = jnp.dot(x, w, preferred_element_type=jnp.float32).astype(jnp.bfloat16)
        return y.reshape(here, CAP, w.shape[1])

    contract = (((1,), (1,)), ((), ()))
    head_grads = (
        lax.dot_general(dy, w_out, contract, preferred_element_type=jnp.float32)
        .astype(jnp.bfloat16)
        .reshape(here, CAP, w_out.shape[0])
    )
    mixed, grad_query, grad_key, grad_value = attention(
        project(w_query), project(w_key), project(w_value), head_grads, usable
    )
    out_part = jnp.dot(mixed, w_out, preferred_element_type=jnp.float32)
    grad_part = (
        lax.dot_general(grad_query, w_query, contract, preferred_element_type=jnp.float32)
        + lax.dot_general(grad_key, w_key, contract, preferred_element_type=jnp.float32)
        + lax.dot_general(grad_value, w_value, contract, preferred_element_type=jnp.float32)
    )

    def pieces(part):
        return part.astype(jnp.bfloat16).reshape(here * CAP, tp_count, width)

    parts = jnp.concatenate([pieces(out_part), pieces(grad_part)], axis=2)
    parts = jnp.swapaxes(parts, 0, 1)
    parts = lax.all_to_all(parts, "tp", split_axis=0, concat_axis=0, tiled=True)
    mine = jnp.sum(parts.astype(jnp.float32), axis=0).astype(jnp.bfloat16)
    mine = mine.reshape(here, CAP, 2 * width)
    back = jnp.einsum(
        "crs,crf->scf", choose, mine, preferred_element_type=jnp.float32
    ).astype(jnp.bfloat16)
    back = jnp.swapaxes(back.reshape(seq_count, MOST, here, 2 * width), 1, 2)
    back = lax.all_to_all(back, "seq", split_axis=0, concat_axis=0, tiled=True)
    back = back.reshape(CLUSTERS * MOST, 2 * width)
    result = lax.dot_general(
        spread, back, (((0,), (0,)), ((), ())), preferred_element_type=jnp.float32
    )
    return (result[:, :width].astype(jnp.bfloat16), result[:, width:])


def solution(mesh):
    in_specs = (
        P("seq", "tp"),
        P("seq", None),
        P(None, "tp"),
        P(None, "tp"),
        P(None, "tp"),
        P("tp", None),
        P("seq", "tp"),
    )
    out_specs = (P("seq", "tp"), P("seq", "tp"))
    return jax.shard_map(body, mesh=mesh, in_specs=in_specs, out_specs=out_specs, check_vma=False)
```

```python
import functools

import jax
import jax.numpy as jnp
from jax import lax
from jax.experimental import pallas as pl
from jax.experimental.pallas import tpu as pltpu
from jax.sharding import PartitionSpec as P

MESH = pl.DeviceIdType.MESH
HEAD_DIM = 128
CLUSTERS = 128
CAP = 256
MOST = 8
EMPTY = 128.0
PAIR = 2 * MOST
STRIDE = 27
F32 = jnp.float32
BF16 = jnp.bfloat16


def product(a, b, contract=(1, 0)):
    dims = (((contract[0],), (contract[1],)), ((), ()))
    return lax.dot_general(a, b, dims, preferred_element_type=F32)


def iota(shape, dim):
    return lax.broadcasted_iota(jnp.int32, shape, dim)


def kernel(
    peers,
    ring,
    ids_row,
    ids_col,
    normed,
    grad_out,
    wq_hbm,
    wk_hbm,
    wv_hbm,
    wo_hbm,
    attended,
    grad_normed,
    wq,
    wk,
    wv,
    wo,
    packed,
    recv,
    expanded,
    back,
    xin,
    sums_out,
    sums_in,
    before,
    choose,
    count,
    heads,
    own,
    w_sem,
    go_send,
    go_recv,
    back_send,
    back_recv,
    x_send,
    x_recv,
    r_send,
    r_recv,
):
    s, t = lax.axis_index("seq"), lax.axis_index("tp")
    right, left, across = lax.rem(t + 1, ring), lax.rem(t + ring - 1, ring), lax.rem(t + 2, ring)
    tokens, width = normed.shape
    slots = peers * PAIR
    tile = 256

    weights = [
        pltpu.make_async_copy(src, dst, w_sem.at[i])
        for i, (src, dst) in enumerate(
            ((wq_hbm, wq), (wk_hbm, wk), (wv_hbm, wv), (wo_hbm, wo))
        )
    ]
    for copy in weights:
        copy.start()

    barrier = pltpu.get_barrier_semaphore()

    @pl.loop(1, peers)
    def _(r):
        pl.semaphore_signal(
            barrier, inc=1, device_id=(lax.rem(s + r, peers), t), device_id_type=MESH
        )

    for d in range(1, ring):
        pl.semaphore_signal(
            barrier, inc=1, device_id=(s, lax.rem(t + d, ring)), device_id_type=MESH
        )

    same = ids_col[...] == ids_row[...]
    above = iota((tokens, tokens), 0) < iota((tokens, tokens), 1)
    below = iota((tokens, tokens), 0) > iota((tokens, tokens), 1)
    rank_row = jnp.sum(jnp.where(same & above, 1.0, 0.0), axis=0, keepdims=True)
    rank_col = jnp.sum(jnp.where(same & below, 1.0, 0.0), axis=1, keepdims=True)

    def place(ids, rank):
        return ((ids & 1) * peers + (ids >> 1)) * PAIR + rank.astype(jnp.int32)

    place_row = place(ids_row[...], rank_row)
    place_col = place(ids_col[...], rank_col)

    def pack(half):
        @pl.loop(0, slots // tile)
        def _(i):
            row = iota((tile, tokens), 0) + (half * slots + i * tile)
            put = (row == place_row).astype(F32)
            put_grad = (row == place_row + MOST).astype(BF16)
            filled = jnp.sum(put, axis=1, keepdims=True)
            rows = product(put.astype(BF16), normed[...]) + product(put_grad, grad_out[...])
            lane = iota((tile, width), 1)
            odd = lax.rem(iota((tile, width), 0), PAIR)
            mark = (odd < MOST) & (lane < 128) & (filled < 0.5)
            rows = jnp.where(mark, EMPTY, rows).astype(BF16)
            packed[half, pl.ds(i * (tile // PAIR), tile // PAIR)] = rows.reshape(
                tile // PAIR, PAIR, width
            )

    def send_all(half, src, dst, send_sem, recv_sem):
        pltpu.make_async_copy(src.at[half, s], dst.at[half, s], recv_sem.at[half]).start()

        @pl.loop(1, peers)
        def _(r):
            peer = lax.rem(s + r * STRIDE, peers)
            pltpu.make_async_remote_copy(
                src_ref=src.at[half, peer],
                dst_ref=dst.at[half, s],
                send_sem=send_sem.at[half],
                recv_sem=recv_sem.at[half],
                device_id=(peer, t),
                device_id_type=MESH,
            ).start()

    def wait_all(half, dst, recv_sem):
        pltpu.make_async_copy(dst.at[half], dst.at[half], recv_sem.at[half]).wait()

    def wait_sent(half, src, send_sem):
        part = src.at[half, pl.ds(0, peers - 1)]
        pltpu.make_async_copy(part, part, send_sem.at[half]).wait()

    def hop(src, dst, send_sem, recv_sem, target):
        return pltpu.make_async_remote_copy(
            src_ref=src,
            dst_ref=dst,
            send_sem=send_sem,
            recv_sem=recv_sem,
            device_id=(s, target),
            device_id_type=MESH,
        )

    def gather_hops(half):
        def one(i, src, dst, target):
            return hop(src, dst, x_send.at[half, i], x_recv.at[half, i], target)

        return (
            one(0, xin.at[half, 0], xin.at[half, 1], right),
            one(1, xin.at[half, 0], xin.at[half, 2], left),
            one(2, xin.at[half, 1, 0], xin.at[half, 3, 0], right),
            one(3, xin.at[half, 2, 1], xin.at[half, 3, 1], left),
        )

    def sum_hops(half):
        targets = (right, left, right, left, right, left)
        return [
            hop(
                sums_out.at[half, i],
                sums_in.at[half, i],
                r_send.at[half, i],
                r_recv.at[half, i],
                target,
            )
            for i, target in enumerate(targets)
        ]

    def compact(half):
        wait_all(half, recv, go_recv)
        first = recv[half, :, :, :128].astype(F32)
        valid = (first[:, :MOST] < 0.5 * EMPTY).astype(F32)
        zero = jnp.zeros_like(valid)
        only = jnp.concatenate([valid, zero], axis=1).reshape(slots, 128)
        valid = jnp.concatenate([valid, valid], axis=1).reshape(slots, 128)
        rank = product(before[...], only.astype(BF16))
        count[half] = jnp.broadcast_to(jnp.sum(only, axis=0, keepdims=True), (8, 128))
        second = lax.rem(iota((slots, 128), 0), PAIR) >= MOST
        kept = (valid > 0.5) & (rank < CAP)
        goal = jnp.where(kept, rank + jnp.where(second, CAP * 1.0, 0.0), -1.0).astype(jnp.int32)
        for k in range(2 * CAP // 128):
            choose[half, :, k * 128 : (k + 1) * 128] = (
                goal == iota((slots, 128), 1) + k * 128
            ).astype(BF16)
        rows = recv[half].reshape(slots, width)
        both = product(choose[half], rows, (0, 0)).astype(BF16)
        xin[half, 0] = both.reshape(2, CAP, width)
        hops = gather_hops(half)
        hops[0].start()
        hops[1].start()

    def relay(half):
        hops = gather_hops(half)
        hops[0].wait_recv()
        hops[2].start()
        hops[1].wait_recv()
        hops[3].start()

    def project(half):
        hops = gather_hops(half)
        hops[2].wait_recv()
        hops[3].wait_recv()
        order = (t, left, right, across)
        for i, w in enumerate((wq, wk, wv)):
            total = None
            for k in range(4):
                part = product(xin[half, k, 0], w[pl.ds(order[k] * width, width), :])
                total = part if total is None else total + part
            heads[i] = total.astype(BF16)
        total = None
        for k in range(4):
            columns = pl.ds(pl.multiple_of(order[k] * width, width), width)
            part = product(xin[half, k, 1], wo[:, columns], (1, 1))
            total = part if total is None else total + part
        heads[3] = total.astype(BF16)

    def attend(half):
        scale = HEAD_DIM ** (-0.5)
        usable = count[half, :1, :1] > iota((1, CAP), 1).astype(F32)

        @pl.loop(0, width // HEAD_DIM)
        def _(h):
            at = pl.ds(pl.multiple_of(h * HEAD_DIM, HEAD_DIM), HEAD_DIM)
            query, key_rows, value_rows, grad_rows = (heads[i, :, at] for i in range(4))
            scores = product(query, key_rows, (1, 1)) * scale
            scores = jnp.where(usable, scores, -1e30)
            raised = jnp.exp(scores - jnp.max(scores, axis=1, keepdims=True))
            probs = raised / jnp.sum(raised, axis=1, keepdims=True)
            rounded = probs.astype(BF16)
            grad_probs = product(grad_rows, value_rows, (1, 1))
            inner = jnp.sum(grad_probs * probs, axis=1, keepdims=True)
            grad_scores = (probs * (grad_probs - inner) * scale).astype(BF16)
            heads[4, :, at] = product(rounded, value_rows).astype(BF16)
            heads[5, :, at] = product(grad_scores, key_rows).astype(BF16)
            heads[6, :, at] = product(grad_scores, query, (0, 0)).astype(BF16)
            heads[7, :, at] = product(rounded, grad_rows, (0, 0)).astype(BF16)

    def out_part(target):
        columns = pl.ds(pl.multiple_of(target * width, width), width)
        return product(heads[4], wo[:, columns])

    def grad_part(target):
        rows = pl.ds(target * width, width)
        return (
            product(heads[5], wq[rows, :], (1, 1))
            + product(heads[6], wk[rows, :], (1, 1))
            + product(heads[7], wv[rows, :], (1, 1))
        )

    def outputs(half):
        hops = sum_hops(half)
        for i, part in ((0, out_part(across)), (1, grad_part(across)), (4, grad_part(right)), (5, out_part(left))):
            sums_out[half, i] = part.astype(BF16)
            hops[i].start()
        own[half, 0] = out_part(t)
        own[half, 1] = grad_part(t)
        for i, part in ((2, out_part(right)), (3, grad_part(left))):
            hops[i - 2].wait_recv()
            sums_out[half, i] = (part + sums_in[half, i - 2].astype(F32)).astype(BF16)
            hops[i].start()

    def finish(half):
        hops = sum_hops(half)
        for i in range(2, 6):
            hops[i].wait_recv()
        out = own[half, 0] + sums_in[half, 2].astype(F32) + sums_in[half, 5].astype(F32)
        grad = own[half, 1] + sums_in[half, 3].astype(F32) + sums_in[half, 4].astype(F32)
        both = jnp.concatenate([out.astype(BF16), grad.astype(BF16)], axis=0)

        @pl.loop(0, slots // tile)
        def _(i):
            rows = product(choose[half, pl.ds(i * tile, tile), :], both).astype(BF16)
            expanded[half, pl.ds(i * (tile // PAIR), tile // PAIR)] = rows.reshape(
                tile // PAIR, PAIR, width
            )

        send_all(half, expanded, back, back_send, back_recv)

    def unpack(half):
        wait_all(half, back, back_recv)
        rows = back[half].reshape(slots, width)
        lane = iota((tokens, slots), 1) + half * slots
        out = product((lane == place_col).astype(BF16), rows)
        grad = product((lane == place_col + MOST).astype(BF16), rows)
        if half == 0:
            attended[...] = out.astype(BF16)
            grad_normed[...] = grad
        else:
            attended[...] = (attended[...].astype(F32) + out).astype(BF16)
            grad_normed[...] = grad_normed[...] + grad

    pack(0)
    pl.semaphore_wait(barrier, peers - 1 + ring - 1)
    send_all(0, packed, recv, go_send, go_recv)
    pack(1)
    send_all(1, packed, recv, go_send, go_recv)

    @pl.loop(0, slots // tile)
    def _(i):
        row, column = iota((tile, slots), 0) + i * tile, iota((tile, slots), 1)
        number = (row >> 4) * MOST + (row & (MOST - 1))
        other = (column >> 4) * MOST + (column & (MOST - 1))
        before[pl.ds(i * tile, tile), :] = (other < number).astype(BF16)

    for copy in weights:
        copy.wait()
    compact(0)
    relay(0)
    project(0)
    attend(0)
    compact(1)
    outputs(0)
    relay(1)
    finish(0)
    project(1)
    attend(1)
    outputs(1)
    finish(1)
    unpack(0)
    unpack(1)

    for half in range(2):
        wait_sent(half, packed, go_send)
        wait_sent(half, expanded, back_send)
        for copy in gather_hops(half):
            copy.wait_send()
        for copy in sum_hops(half):
            copy.wait_send()


def body(normed, cluster, w_query, w_key, w_value, w_out, grad_out):
    peers, ring = lax.axis_size("seq"), lax.axis_size("tp")
    tokens, width = normed.shape
    slots = peers * PAIR
    vmem = pl.BlockSpec(memory_space=pltpu.VMEM)
    anywhere = pl.BlockSpec(memory_space=pl.ANY)
    dma = pltpu.SemaphoreType.DMA
    return pl.pallas_call(
        functools.partial(kernel, peers, ring),
        out_shape=(
            jax.ShapeDtypeStruct((tokens, width), BF16),
            jax.ShapeDtypeStruct((tokens, width), F32),
        ),
        in_specs=[vmem] * 4 + [anywhere] * 4,
        out_specs=(vmem, vmem),
        scratch_shapes=[
            pltpu.VMEM(w_query.shape, BF16),
            pltpu.VMEM(w_key.shape, BF16),
            pltpu.VMEM(w_value.shape, BF16),
            pltpu.VMEM(w_out.shape, BF16),
            pltpu.VMEM((2, peers, PAIR, width), BF16),
            pltpu.VMEM((2, peers, PAIR, width), BF16),
            pltpu.VMEM((2, peers, PAIR, width), BF16),
            pltpu.VMEM((2, peers, PAIR, width), BF16),
            pltpu.VMEM((2, ring, 2, CAP, width), BF16),
            pltpu.VMEM((2, 6, CAP, width), BF16),
            pltpu.VMEM((2, 6, CAP, width), BF16),
            pltpu.VMEM((slots, slots), BF16),
            pltpu.VMEM((2, slots, 2 * CAP), BF16),
            pltpu.VMEM((2, 8, 128), F32),
            pltpu.VMEM((8, CAP, width), BF16),
            pltpu.VMEM((2, 2, CAP, width), F32),
            dma((4,)),
            dma((2,)),
            dma((2,)),
            dma((2,)),
            dma((2,)),
            dma((2, 4)),
            dma((2, 4)),
            dma((2, 6)),
            dma((2, 6)),
        ],
        compiler_params=pltpu.CompilerParams(
            collective_id=0, has_side_effects=True, vmem_limit_bytes=60 * 2**20
        ),
        name="routed",
    )(cluster.reshape(1, tokens), cluster, normed, grad_out, w_query, w_key, w_value, w_out)


def solution(mesh):
    in_specs = (
        P("seq", "tp"),
        P("seq", None),
        P(None, "tp"),
        P(None, "tp"),
        P(None, "tp"),
        P("tp", None),
        P("seq", "tp"),
    )
    out_specs = (P("seq", "tp"), P("seq", "tp"))
    return jax.shard_map(body, mesh=mesh, in_specs=in_specs, out_specs=out_specs, check_vma=False)
```

```python
import functools

import jax
import jax.numpy as jnp
from jax import lax
from jax.experimental import pallas as pl
from jax.experimental.pallas import tpu as pltpu
from jax.sharding import PartitionSpec as P

MESH = pl.DeviceIdType.MESH
HEAD_DIM = 128
CLUSTERS = 128
CAP = 256
MOST = 8
EMPTY = 128.0
PAIR = 2 * MOST
STRIDE = 27
PARTS = 2
F32 = jnp.float32
BF16 = jnp.bfloat16


def product(a, b, contract=(1, 0)):
    dims = (((contract[0],), (contract[1],)), ((), ()))
    return lax.dot_general(a, b, dims, preferred_element_type=F32)


def iota(shape, dim):
    return lax.broadcasted_iota(jnp.int32, shape, dim)


def kernel(
    peers,
    ring,
    ids_row,
    normed,
    grad_out,
    wq_hbm,
    wk_hbm,
    wv_hbm,
    wo_hbm,
    attended,
    grad_normed,
    wq,
    wk,
    wv,
    wo,
    packed,
    recv,
    expanded,
    back,
    xin,
    sums_out,
    sums_in,
    before,
    choose,
    gather_rows,
    take,
    count,
    heads,
    total,
    own,
    w_sem,
    go_send,
    go_recv,
    back_send,
    back_recv,
    x_send,
    x_recv,
    r_send,
    r_recv,
):
    s, t = lax.axis_index("seq"), lax.axis_index("tp")
    right, left, across = lax.rem(t + 1, ring), lax.rem(t + ring - 1, ring), lax.rem(t + 2, ring)
    tokens, width = normed.shape
    part_width = width // PARTS
    slots = peers * PAIR
    tile = 256

    weights = [
        pltpu.make_async_copy(src, dst, w_sem.at[i])
        for i, (src, dst) in enumerate(
            ((wq_hbm, wq), (wk_hbm, wk), (wv_hbm, wv), (wo_hbm, wo))
        )
    ]
    for copy in weights:
        copy.start()

    barrier = pltpu.get_barrier_semaphore()

    @pl.loop(1, peers)
    def _(r):
        pl.semaphore_signal(
            barrier, inc=1, device_id=(lax.rem(s + r, peers), t), device_id_type=MESH
        )

    for d in range(1, ring):
        pl.semaphore_signal(
            barrier, inc=1, device_id=(s, lax.rem(t + d, ring)), device_id_type=MESH
        )

    def column(row):
        wide = jnp.broadcast_to(row.astype(F32), (128, tokens))
        blocks = [jnp.transpose(wide[:, i : i + 128]) for i in range(0, tokens, 128)]
        return jnp.concatenate(blocks, axis=0)[:, :1].astype(jnp.int32)

    same = column(ids_row[...]) == ids_row[...]
    above = iota((tokens, tokens), 0) < iota((tokens, tokens), 1)
    rank_row = jnp.sum(jnp.where(same & above, 1.0, 0.0), axis=0, keepdims=True)
    place_row = ((ids_row[...] & 1) * peers + (ids_row[...] >> 1)) * PAIR + rank_row.astype(
        jnp.int32
    )

    def pack(half):
        @pl.loop(0, slots // tile)
        def _(i):
            row = iota((tile, tokens), 0) + (half * slots + i * tile)
            put = (row == place_row).astype(F32)
            put_grad = (row == place_row + MOST).astype(BF16)
            filled = jnp.sum(put, axis=1, keepdims=True)
            rows = product(put.astype(BF16), normed[...]) + product(put_grad, grad_out[...])
            odd = lax.rem(iota((tile, 128), 0), PAIR)
            mark = (odd < MOST) & (filled < 0.5)
            first = jnp.where(mark, EMPTY, rows[:, :128])
            rows = jnp.concatenate([first, rows[:, 128:]], axis=1).astype(BF16)
            for part in range(PARTS):
                some = rows[:, part * part_width : (part + 1) * part_width]
                packed[half, part, pl.ds(i * (tile // PAIR), tile // PAIR)] = some.reshape(
                    tile // PAIR, PAIR, part_width
                )

    def send_all(half, part, src, dst, send_sem, recv_sem):
        pltpu.make_async_copy(
            src.at[half, part, s], dst.at[half, part, s], recv_sem.at[half, part]
        ).start()

        @pl.loop(1, peers)
        def _(r):
            peer = lax.rem(s + r * STRIDE, peers)
            pltpu.make_async_remote_copy(
                src_ref=src.at[half, part, peer],
                dst_ref=dst.at[half, part, s],
                send_sem=send_sem.at[half, part],
                recv_sem=recv_sem.at[half, part],
                device_id=(peer, t),
                device_id_type=MESH,
            ).start()

    def wait_all(half, part, dst, recv_sem):
        everything = dst.at[half, part]
        pltpu.make_async_copy(everything, everything, recv_sem.at[half, part]).wait()

    def wait_sent(half, part, src, send_sem):
        others = src.at[half, part, pl.ds(0, peers - 1)]
        pltpu.make_async_copy(others, others, send_sem.at[half, part]).wait()

    def hop(src, dst, send_sem, recv_sem, target):
        return pltpu.make_async_remote_copy(
            src_ref=src,
            dst_ref=dst,
            send_sem=send_sem,
            recv_sem=recv_sem,
            device_id=(s, target),
            device_id_type=MESH,
        )

    def gather_hop(half, part, i):
        block = xin.at[half, part]
        src, dst, target = (
            (block.at[0], block.at[1], right),
            (block.at[0], block.at[2], left),
            (block.at[1, 0], block.at[3, 0], right),
            (block.at[2, 1], block.at[3, 1], left),
        )[i]
        return hop(src, dst, x_send.at[half, part, i], x_recv.at[half, part, i], target)

    def sum_hop(half, part, i):
        return hop(
            sums_out.at[half, part, i],
            sums_in.at[half, part, i],
            r_send.at[half, part, i],
            r_recv.at[half, part, i],
            (right, left)[i % 2],
        )

    def rank_slots(half):
        first = recv[half, 0, :, :, :128].astype(F32)
        valid = (first[:, :MOST] < 0.5 * EMPTY).astype(F32)
        zero = jnp.zeros_like(valid)
        only = jnp.concatenate([valid, zero], axis=1).reshape(slots, 128)
        valid = jnp.concatenate([valid, valid], axis=1).reshape(slots, 128)
        rank = product(before[...], only.astype(BF16))
        count[half] = jnp.broadcast_to(jnp.sum(only, axis=0, keepdims=True), (8, 128))
        second = lax.rem(iota((slots, 128), 0), PAIR) >= MOST
        kept = (valid > 0.5) & (rank < CAP)
        goal = jnp.where(kept, rank + jnp.where(second, CAP * 1.0, 0.0), -1.0)
        blocks = [jnp.transpose(goal[i : i + 128]) for i in range(0, slots, 128)]
        goal_row = jnp.concatenate(blocks, axis=1)[:1].astype(jnp.int32)
        goal = goal.astype(jnp.int32)
        for k in range(0, 2 * CAP, 128):
            choose[half, :, k : k + 128] = (goal == iota((slots, 128), 1) + k).astype(BF16)
            gather_rows[half, k : k + 128] = (goal_row == iota((128, slots), 0) + k).astype(BF16)

    def compact(half, part):
        wait_all(half, part, recv, go_recv)
        if part == 0:
            rank_slots(half)
        rows = recv[half, part].reshape(slots, part_width)
        both = product(gather_rows[half], rows).astype(BF16)
        xin[half, part, 0] = both.reshape(2, CAP, part_width)
        gather_hop(half, part, 0).start()
        gather_hop(half, part, 1).start()

    def relay(half, part):
        gather_hop(half, part, 0).wait_recv()
        gather_hop(half, part, 2).start()
        gather_hop(half, part, 1).wait_recv()
        gather_hop(half, part, 3).start()

    def project(half, part):
        gather_hop(half, part, 2).wait_recv()
        gather_hop(half, part, 3).wait_recv()
        starts = [
            pl.multiple_of(owner * width + part * part_width, part_width)
            for owner in (t, left, right, across)
        ]

        def add(i, value):
            if part > 0:
                value = total[i] + value
            if part < PARTS - 1:
                total[i] = value
            else:
                heads[i] = value.astype(BF16)

        for i, w in enumerate((wq, wk, wv)):
            value = None
            for k in range(4):
                more = product(xin[half, part, k, 0], w[pl.ds(starts[k], part_width), :])
                value = more if value is None else value + more
            add(i, value)
        value = None
        for k in range(4):
            more = product(xin[half, part, k, 1], wo[:, pl.ds(starts[k], part_width)], (1, 1))
            value = more if value is None else value + more
        add(3, value)

    def attend(half):
        scale = HEAD_DIM ** (-0.5)
        usable = count[half, :1, :1] > iota((1, CAP), 1).astype(F32)

        @pl.loop(0, width // HEAD_DIM)
        def _(h):
            at = pl.ds(pl.multiple_of(h * HEAD_DIM, HEAD_DIM), HEAD_DIM)
            query, key_rows, value_rows, grad_rows = (heads[i, :, at] for i in range(4))
            scores = product(query, key_rows, (1, 1)) * scale
            scores = jnp.where(usable, scores, -1e30)
            raised = jnp.exp(scores - jnp.max(scores, axis=1, keepdims=True))
            probs = raised / jnp.sum(raised, axis=1, keepdims=True)
            rounded = probs.astype(BF16)
            grad_probs = product(grad_rows, value_rows, (1, 1))
            inner = jnp.sum(grad_probs * probs, axis=1, keepdims=True)
            grad_scores = (probs * (grad_probs - inner) * scale).astype(BF16)
            heads[4, :, at] = product(rounded, value_rows).astype(BF16)
            heads[5, :, at] = product(grad_scores, key_rows).astype(BF16)
            heads[6, :, at] = product(grad_scores, query, (0, 0)).astype(BF16)
            heads[7, :, at] = product(rounded, grad_rows, (0, 0)).astype(BF16)

    def out_part(target, part):
        start = pl.multiple_of(target * width + part * part_width, part_width)
        return product(heads[4], wo[:, pl.ds(start, part_width)])

    def grad_part(target, part):
        start = pl.multiple_of(target * width + part * part_width, part_width)
        rows = pl.ds(start, part_width)
        return (
            product(heads[5], wq[rows, :], (1, 1))
            + product(heads[6], wk[rows, :], (1, 1))
            + product(heads[7], wv[rows, :], (1, 1))
        )

    def outputs(half, part):
        for i, target, make in (
            (0, across, out_part),
            (1, across, grad_part),
            (4, right, grad_part),
            (5, left, out_part),
        ):
            sums_out[half, part, i] = make(target, part).astype(BF16)
            sum_hop(half, part, i).start()
        own[half, part, 2] = out_part(right, part)
        own[half, part, 3] = grad_part(left, part)
        own[half, part, 0] = out_part(t, part)
        own[half, part, 1] = grad_part(t, part)

    def combine(half, part):
        for i in (2, 3):
            sum_hop(half, part, i - 2).wait_recv()
            more = sums_in[half, part, i - 2].astype(F32)
            sums_out[half, part, i] = (own[half, part, i] + more).astype(BF16)
            sum_hop(half, part, i).start()

    def finish(half, part):
        for i in range(2, 6):
            sum_hop(half, part, i).wait_recv()
        arrived = [sums_in[half, part, i].astype(F32) for i in range(2, 6)]
        out = own[half, part, 0] + arrived[0] + arrived[3]
        grad = own[half, part, 1] + arrived[1] + arrived[2]
        both = jnp.concatenate([out.astype(BF16), grad.astype(BF16)], axis=0)

        @pl.loop(0, slots // tile)
        def _(i):
            rows = product(choose[half, pl.ds(i * tile, tile), :], both).astype(BF16)
            expanded[half, part, pl.ds(i * (tile // PAIR), tile // PAIR)] = rows.reshape(
                tile // PAIR, PAIR, part_width
            )

        send_all(half, part, expanded, back, back_send, back_recv)

    def unpack(half, part):
        wait_all(half, part, back, back_recv)
        rows = back[half, part].reshape(slots, part_width)
        at = pl.ds(part * part_width, part_width)
        out = product(take[half, 0], rows)
        grad = product(take[half, 1], rows)
        if half == 0:
            attended[:, at] = out.astype(BF16)
            grad_normed[:, at] = grad
        else:
            attended[:, at] = (attended[:, at].astype(F32) + out).astype(BF16)
            grad_normed[:, at] = grad_normed[:, at] + grad

    everything = [(half, part) for half in range(2) for part in range(PARTS)]
    pack(0)
    pl.semaphore_wait(barrier, peers - 1 + ring - 1)
    for part in range(PARTS):
        send_all(0, part, packed, recv, go_send, go_recv)
    pack(1)
    for part in range(PARTS):
        send_all(1, part, packed, recv, go_send, go_recv)

    @pl.loop(0, slots // tile)
    def _(i):
        row, other_row = iota((tile, slots), 0) + i * tile, iota((tile, slots), 1)
        number = (row >> 4) * MOST + (row & (MOST - 1))
        other = (other_row >> 4) * MOST + (other_row & (MOST - 1))
        before[pl.ds(i * tile, tile), :] = (other < number).astype(BF16)

    place_column = column(place_row)
    for half in range(2):
        lane = iota((tokens, slots), 1) + half * slots
        take[half, 0] = (lane == place_column).astype(BF16)
        take[half, 1] = (lane == place_column + MOST).astype(BF16)

    for copy in weights:
        copy.wait()

    compact(0, 0)
    relay(0, 0)
    compact(0, 1)
    project(0, 0)
    relay(0, 1)
    compact(1, 0)
    project(0, 1)
    relay(1, 0)
    attend(0)
    outputs(0, 0)
    compact(1, 1)
    combine(0, 0)
    outputs(0, 1)
    relay(1, 1)
    finish(0, 0)
    combine(0, 1)
    project(1, 0)
    finish(0, 1)
    project(1, 1)
    attend(1)
    outputs(1, 0)
    outputs(1, 1)
    combine(1, 0)
    combine(1, 1)
    finish(1, 0)
    finish(1, 1)
    for half, part in everything:
        unpack(half, part)

    for half, part in everything:
        wait_sent(half, part, packed, go_send)
        wait_sent(half, part, expanded, back_send)
        for i in range(4):
            gather_hop(half, part, i).wait_send()
        for i in range(6):
            sum_hop(half, part, i).wait_send()


def body(normed, cluster, w_query, w_key, w_value, w_out, grad_out):
    peers, ring = lax.axis_size("seq"), lax.axis_size("tp")
    tokens, width = normed.shape
    slots = peers * PAIR
    part_width = width // PARTS
    vmem = pl.BlockSpec(memory_space=pltpu.VMEM)
    anywhere = pl.BlockSpec(memory_space=pl.ANY)
    dma = pltpu.SemaphoreType.DMA
    return pl.pallas_call(
        functools.partial(kernel, peers, ring),
        out_shape=(
            jax.ShapeDtypeStruct((tokens, width), BF16),
            jax.ShapeDtypeStruct((tokens, width), F32),
        ),
        in_specs=[vmem] * 3 + [anywhere] * 4,
        out_specs=(vmem, vmem),
        scratch_shapes=[
            pltpu.VMEM(w_query.shape, BF16),
            pltpu.VMEM(w_key.shape, BF16),
            pltpu.VMEM(w_value.shape, BF16),
            pltpu.VMEM(w_out.shape, BF16),
            pltpu.VMEM((2, PARTS, peers, PAIR, part_width), BF16),
            pltpu.VMEM((2, PARTS, peers, PAIR, part_width), BF16),
            pltpu.VMEM((2, PARTS, peers, PAIR, part_width), BF16),
            pltpu.VMEM((2, PARTS, peers, PAIR, part_width), BF16),
            pltpu.VMEM((2, PARTS, ring, 2, CAP, part_width), BF16),
            pltpu.VMEM((2, PARTS, 6, CAP, part_width), BF16),
            pltpu.VMEM((2, PARTS, 6, CAP, part_width), BF16),
            pltpu.VMEM((slots, slots), BF16),
            pltpu.VMEM((2, slots, 2 * CAP), BF16),
            pltpu.VMEM((2, 2 * CAP, slots), BF16),
            pltpu.VMEM((2, 2, tokens, slots), BF16),
            pltpu.VMEM((2, 8, 128), F32),
            pltpu.VMEM((8, CAP, width), BF16),
            pltpu.VMEM((4, CAP, width), F32),
            pltpu.VMEM((2, PARTS, 4, CAP, part_width), F32),
            dma((4,)),
            dma((2, PARTS)),
            dma((2, PARTS)),
            dma((2, PARTS)),
            dma((2, PARTS)),
            dma((2, PARTS, 4)),
            dma((2, PARTS, 4)),
            dma((2, PARTS, 6)),
            dma((2, PARTS, 6)),
        ],
        compiler_params=pltpu.CompilerParams(
            collective_id=0, has_side_effects=True, vmem_limit_bytes=60 * 2**20
        ),
        name="routed",
    )(cluster.reshape(1, tokens), normed, grad_out, w_query, w_key, w_value, w_out)


def solution(mesh):
    in_specs = (
        P("seq", "tp"),
        P("seq", None),
        P(None, "tp"),
        P(None, "tp"),
        P(None, "tp"),
        P("tp", None),
        P("seq", "tp"),
    )
    out_specs = (P("seq", "tp"), P("seq", "tp"))
    return jax.shard_map(body, mesh=mesh, in_specs=in_specs, out_specs=out_specs, check_vma=False)
```

```python
import functools

import jax
import jax.numpy as jnp
from jax import lax
from jax.experimental import pallas as pl
from jax.experimental.pallas import tpu as pltpu
from jax.sharding import PartitionSpec as P

MESH = pl.DeviceIdType.MESH
HEAD_DIM = 128
CLUSTERS = 128
CAP = 256
MOST = 8
EMPTY = 128.0
PAIR = 2 * MOST
STRIDE = 27
PARTS = 2
F32 = jnp.float32
BF16 = jnp.bfloat16


def product(a, b, contract=(1, 0)):
    dims = (((contract[0],), (contract[1],)), ((), ()))
    return lax.dot_general(a, b, dims, preferred_element_type=F32)


def iota(shape, dim):
    return lax.broadcasted_iota(jnp.int32, shape, dim)


def kernel(
    peers,
    ring,
    ids_row,
    normed,
    grad_out,
    wq_hbm,
    wk_hbm,
    wv_hbm,
    wo_hbm,
    result,
    wq,
    wk,
    wv,
    wo,
    packed,
    recv,
    expanded,
    back,
    xin,
    sums_out,
    sums_in,
    before,
    choose,
    gather_rows,
    take,
    count,
    heads,
    total,
    own,
    w_sem,
    go_send,
    go_recv,
    back_send,
    back_recv,
    x_send,
    x_recv,
    r_send,
    r_recv,
):
    s, t = lax.axis_index("seq"), lax.axis_index("tp")
    right, left, across = lax.rem(t + 1, ring), lax.rem(t + ring - 1, ring), lax.rem(t + 2, ring)
    tokens, width = normed.shape
    part_width = width // PARTS
    slots = peers * PAIR
    tile = 256

    weights = [
        pltpu.make_async_copy(src, dst, w_sem.at[i])
        for i, (src, dst) in enumerate(
            ((wq_hbm, wq), (wk_hbm, wk), (wv_hbm, wv), (wo_hbm, wo))
        )
    ]
    for copy in weights:
        copy.start()

    barrier = pltpu.get_barrier_semaphore()

    @pl.loop(1, peers)
    def _(r):
        pl.semaphore_signal(
            barrier, inc=1, device_id=(lax.rem(s + r, peers), t), device_id_type=MESH
        )

    for d in range(1, ring):
        pl.semaphore_signal(
            barrier, inc=1, device_id=(s, lax.rem(t + d, ring)), device_id_type=MESH
        )

    def column(row):
        wide = jnp.broadcast_to(row.astype(F32), (128, tokens))
        blocks = [jnp.transpose(wide[:, i : i + 128]) for i in range(0, tokens, 128)]
        return jnp.concatenate(blocks, axis=0)[:, :1].astype(jnp.int32)

    same = column(ids_row[...]) == ids_row[...]
    above = iota((tokens, tokens), 0) < iota((tokens, tokens), 1)
    rank_row = jnp.sum(jnp.where(same & above, 1.0, 0.0), axis=0, keepdims=True)
    place_row = ((ids_row[...] & 1) * peers + (ids_row[...] >> 1)) * PAIR + rank_row.astype(
        jnp.int32
    )

    def pack(half):
        @pl.loop(0, slots // tile)
        def _(i):
            row = iota((tile, tokens), 0) + (half * slots + i * tile)
            put = (row == place_row).astype(F32)
            put_grad = (row == place_row + MOST).astype(BF16)
            filled = jnp.sum(put, axis=1, keepdims=True)
            rows = product(put.astype(BF16), normed[...]) + product(put_grad, grad_out[...])
            odd = lax.rem(iota((tile, 128), 0), PAIR)
            mark = (odd < MOST) & (filled < 0.5)
            first = jnp.where(mark, EMPTY, rows[:, :128])
            rows = jnp.concatenate([first, rows[:, 128:]], axis=1).astype(BF16)
            for part in range(PARTS):
                some = rows[:, part * part_width : (part + 1) * part_width]
                packed[half, part, pl.ds(i * (tile // PAIR), tile // PAIR)] = some.reshape(
                    tile // PAIR, PAIR, part_width
                )

    def send_all(half, part, src, dst, send_sem, recv_sem):
        pltpu.make_async_copy(
            src.at[half, part, s], dst.at[half, part, s], recv_sem.at[half, part]
        ).start()

        @pl.loop(1, peers)
        def _(r):
            peer = lax.rem(s + r * STRIDE, peers)
            pltpu.make_async_remote_copy(
                src_ref=src.at[half, part, peer],
                dst_ref=dst.at[half, part, s],
                send_sem=send_sem.at[half, part],
                recv_sem=recv_sem.at[half, part],
                device_id=(peer, t),
                device_id_type=MESH,
            ).start()

    def wait_all(half, part, dst, recv_sem):
        everything = dst.at[half, part]
        pltpu.make_async_copy(everything, everything, recv_sem.at[half, part]).wait()

    def wait_sent(half, part, src, send_sem):
        others = src.at[half, part, pl.ds(0, peers - 1)]
        pltpu.make_async_copy(others, others, send_sem.at[half, part]).wait()

    def hop(src, dst, send_sem, recv_sem, target):
        return pltpu.make_async_remote_copy(
            src_ref=src,
            dst_ref=dst,
            send_sem=send_sem,
            recv_sem=recv_sem,
            device_id=(s, target),
            device_id_type=MESH,
        )

    def gather_hop(half, part, i):
        block = xin.at[half, part]
        src, dst, target = (
            (block.at[0], block.at[1], right),
            (block.at[0], block.at[2], left),
            (block.at[1, 0], block.at[3, 0], right),
            (block.at[2, 1], block.at[3, 1], left),
        )[i]
        return hop(src, dst, x_send.at[half, part, i], x_recv.at[half, part, i], target)

    def sum_hop(half, part, i):
        target = (right, left)[i % 2]
        return hop(
            sums_out.at[half, part, i],
            sums_in.at[half, part, i],
            r_send.at[half, part, i],
            r_recv.at[half, part, i],
            target,
        )

    def rank_slots(half):
        first = recv[half, 0, :, :, :128].astype(F32)
        valid = (first[:, :MOST] < 0.5 * EMPTY).astype(F32)
        zero = jnp.zeros_like(valid)
        only = jnp.concatenate([valid, zero], axis=1).reshape(slots, 128)
        valid = jnp.concatenate([valid, valid], axis=1).reshape(slots, 128)
        rank = product(before[...], only.astype(BF16))
        count[half] = jnp.broadcast_to(jnp.sum(only, axis=0, keepdims=True), (8, 128))
        second = lax.rem(iota((slots, 128), 0), PAIR) >= MOST
        kept = (valid > 0.5) & (rank < CAP)
        goal = jnp.where(kept, rank + jnp.where(second, CAP * 1.0, 0.0), -1.0)
        blocks = [jnp.transpose(goal[i : i + 128]) for i in range(0, slots, 128)]
        goal_row = jnp.concatenate(blocks, axis=1)[:1].astype(jnp.int32)
        goal = goal.astype(jnp.int32)
        for k in range(0, 2 * CAP, 128):
            choose[half, :, k : k + 128] = (goal == iota((slots, 128), 1) + k).astype(BF16)
            gather_rows[half, k : k + 128] = (goal_row == iota((128, slots), 0) + k).astype(BF16)

    def compact(half, part):
        wait_all(half, part, recv, go_recv)
        if part == 0:
            rank_slots(half)
        rows = recv[half, part].reshape(slots, part_width)
        both = product(gather_rows[half], rows).astype(BF16)
        xin[half, part, 0] = both.reshape(2, CAP, part_width)
        for i in range(2):
            gather_hop(half, part, i).start()

    def relay(half, part):
        for i in range(2):
            gather_hop(half, part, i).wait_recv()
            gather_hop(half, part, 2 + i).start()

    def project(half, part):
        gather_hop(half, part, 2).wait_recv()
        gather_hop(half, part, 3).wait_recv()
        starts = [
            pl.multiple_of(owner * width + part * part_width, part_width)
            for owner in (t, left, right, across)
        ]

        def add(i, value):
            if part > 0:
                value = total[i] + value
            if part < PARTS - 1:
                total[i] = value
            else:
                heads[i] = value.astype(BF16)

        for i, w in enumerate((wq, wk, wv)):
            value = None
            for k in range(4):
                more = product(xin[half, part, k, 0], w[pl.ds(starts[k], part_width), :])
                value = more if value is None else value + more
            add(i, value)
        value = None
        for k in range(4):
            more = product(xin[half, part, k, 1], wo[:, pl.ds(starts[k], part_width)], (1, 1))
            value = more if value is None else value + more
        add(3, value)

    def attend(half):
        scale = HEAD_DIM ** (-0.5)
        usable = count[half, :1, :1] > iota((1, CAP), 1).astype(F32)

        @pl.loop(0, width // HEAD_DIM, unroll=4)
        def _(h):
            at = pl.ds(pl.multiple_of(h * HEAD_DIM, HEAD_DIM), HEAD_DIM)
            query, key_rows, value_rows, grad_rows = (heads[i, :, at] for i in range(4))
            scores = product(query, key_rows, (1, 1)) * scale
            scores = jnp.where(usable, scores, -1e30)
            raised = jnp.exp(scores - jnp.max(scores, axis=1, keepdims=True))
            probs = raised / jnp.sum(raised, axis=1, keepdims=True)
            rounded = probs.astype(BF16)
            grad_probs = product(grad_rows, value_rows, (1, 1))
            inner = jnp.sum(grad_probs * probs, axis=1, keepdims=True)
            grad_scores = (probs * (grad_probs - inner) * scale).astype(BF16)
            heads[4, :, at] = product(rounded, value_rows).astype(BF16)
            heads[5, :, at] = product(grad_scores, key_rows).astype(BF16)
            heads[6, :, at] = product(grad_scores, query, (0, 0)).astype(BF16)
            heads[7, :, at] = product(rounded, grad_rows, (0, 0)).astype(BF16)

    def out_part(target, part):
        start = pl.multiple_of(target * width + part * part_width, part_width)
        return product(heads[4], wo[:, pl.ds(start, part_width)])

    def grad_part(target, part):
        start = pl.multiple_of(target * width + part * part_width, part_width)
        rows = pl.ds(start, part_width)
        return (
            product(heads[5], wq[rows, :], (1, 1))
            + product(heads[6], wk[rows, :], (1, 1))
            + product(heads[7], wv[rows, :], (1, 1))
        )

    def outputs(half, part):
        for i, target, make in (
            (0, across, out_part),
            (1, across, grad_part),
            (4, right, grad_part),
            (5, left, out_part),
        ):
            sums_out[half, part, i] = make(target, part).astype(BF16)
            sum_hop(half, part, i).start()
        for i, target, make in ((2, right, out_part), (3, left, grad_part)):
            own[half, part, i] = make(target, part)
        own[half, part, 0] = out_part(t, part)
        own[half, part, 1] = grad_part(t, part)

    def combine(half, part):
        for i in (2, 3):
            sum_hop(half, part, i - 2).wait_recv()
            more = sums_in[half, part, i - 2].astype(F32)
            sums_out[half, part, i] = (own[half, part, i] + more).astype(BF16)
            sum_hop(half, part, i).start()

    def finish(half, part):
        for i in range(2, 6):
            sum_hop(half, part, i).wait_recv()
        out, grad = own[half, part, 0], own[half, part, 1]
        for i in range(2, 6):
            more = sums_in[half, part, i].astype(F32)
            if i in (2, 5):
                out = out + more
            else:
                grad = grad + more
        both = jnp.concatenate([out.astype(BF16), grad.astype(BF16)], axis=0)

        @pl.loop(0, slots // tile)
        def _(i):
            rows = product(choose[half, pl.ds(i * tile, tile), :], both).astype(BF16)
            expanded[half, part, pl.ds(i * (tile // PAIR), tile // PAIR)] = rows.reshape(
                tile // PAIR, PAIR, part_width
            )

        send_all(half, part, expanded, back, back_send, back_recv)

    def unpack(half, part):
        wait_all(half, part, back, back_recv)
        rows = back[half, part].reshape(slots, part_width)
        at = pl.ds(part * part_width, part_width)
        out = product(take[half, 0], rows)
        grad = product(take[half, 1], rows)
        for i, value in enumerate((out, grad)):
            if half == 1:
                value = result[i, :, at].astype(F32) + value
            result[i, :, at] = value.astype(BF16)

    everything = [(half, part) for half in range(2) for part in range(PARTS)]
    pack(0)
    pl.semaphore_wait(barrier, peers - 1 + ring - 1)
    for part in range(PARTS):
        send_all(0, part, packed, recv, go_send, go_recv)
    pack(1)
    for part in range(PARTS):
        send_all(1, part, packed, recv, go_send, go_recv)

    @pl.loop(0, slots // tile)
    def _(i):
        row, other_row = iota((tile, slots), 0) + i * tile, iota((tile, slots), 1)
        number = (row >> 4) * MOST + (row & (MOST - 1))
        other = (other_row >> 4) * MOST + (other_row & (MOST - 1))
        before[pl.ds(i * tile, tile), :] = (other < number).astype(BF16)

    place_column = column(place_row)
    for half in range(2):
        lane = iota((tokens, slots), 1) + half * slots
        take[half, 0] = (lane == place_column).astype(BF16)
        take[half, 1] = (lane == place_column + MOST).astype(BF16)

    for copy in weights:
        copy.wait()

    compact(0, 0)
    compact(0, 1)
    relay(0, 0)
    relay(0, 1)
    compact(1, 0)
    project(0, 0)
    project(0, 1)
    attend(0)
    outputs(0, 0)
    outputs(0, 1)
    combine(0, 0)
    compact(1, 1)
    finish(0, 0)
    combine(0, 1)
    relay(1, 0)
    relay(1, 1)
    finish(0, 1)
    project(1, 0)
    project(1, 1)
    attend(1)
    outputs(1, 0)
    combine(1, 0)
    outputs(1, 1)
    finish(1, 0)
    unpack(0, 0)
    unpack(0, 1)
    combine(1, 1)
    finish(1, 1)
    unpack(1, 0)
    unpack(1, 1)

    for half, part in everything:
        wait_sent(half, part, packed, go_send)
        wait_sent(half, part, expanded, back_send)
        for i in range(4):
            gather_hop(half, part, i).wait_send()
        for i in range(6):
            sum_hop(half, part, i).wait_send()


def body(normed, cluster, w_query, w_key, w_value, w_out, grad_out):
    peers, ring = lax.axis_size("seq"), lax.axis_size("tp")
    tokens, width = normed.shape
    slots = peers * PAIR
    part_width = width // PARTS
    vmem = pl.BlockSpec(memory_space=pltpu.VMEM)
    anywhere = pl.BlockSpec(memory_space=pl.ANY)
    dma = pltpu.SemaphoreType.DMA
    result = pl.pallas_call(
        functools.partial(kernel, peers, ring),
        out_shape=jax.ShapeDtypeStruct((2, tokens, width), BF16),
        in_specs=[vmem] * 3 + [anywhere] * 4,
        out_specs=vmem,
        scratch_shapes=[
            pltpu.VMEM(w_query.shape, BF16),
            pltpu.VMEM(w_key.shape, BF16),
            pltpu.VMEM(w_value.shape, BF16),
            pltpu.VMEM(w_out.shape, BF16),
            pltpu.VMEM((2, PARTS, peers, PAIR, part_width), BF16),
            pltpu.VMEM((2, PARTS, peers, PAIR, part_width), BF16),
            pltpu.VMEM((2, PARTS, peers, PAIR, part_width), BF16),
            pltpu.VMEM((2, PARTS, peers, PAIR, part_width), BF16),
            pltpu.VMEM((2, PARTS, ring, 2, CAP, part_width), BF16),
            pltpu.VMEM((2, PARTS, 6, CAP, part_width), BF16),
            pltpu.VMEM((2, PARTS, 6, CAP, part_width), BF16),
            pltpu.VMEM((slots, slots), BF16),
            pltpu.VMEM((2, slots, 2 * CAP), BF16),
            pltpu.VMEM((2, 2 * CAP, slots), BF16),
            pltpu.VMEM((2, 2, tokens, slots), BF16),
            pltpu.VMEM((2, 8, 128), F32),
            pltpu.VMEM((8, CAP, width), BF16),
            pltpu.VMEM((4, CAP, width), F32),
            pltpu.VMEM((2, PARTS, 4, CAP, part_width), F32),
            dma((4,)),
            dma((2, PARTS)),
            dma((2, PARTS)),
            dma((2, PARTS)),
            dma((2, PARTS)),
            dma((2, PARTS, 4)),
            dma((2, PARTS, 4)),
            dma((2, PARTS, 6)),
            dma((2, PARTS, 6)),
        ],
        compiler_params=pltpu.CompilerParams(
            collective_id=0, has_side_effects=True, vmem_limit_bytes=60 * 2**20
        ),
        name="routed",
    )(cluster.reshape(1, tokens), normed, grad_out, w_query, w_key, w_value, w_out)
    return (result[0], result[1].astype(F32))


def solution(mesh):
    in_specs = (
        P("seq", "tp"),
        P("seq", None),
        P(None, "tp"),
        P(None, "tp"),
        P(None, "tp"),
        P("tp", None),
        P("seq", "tp"),
    )
    out_specs = (P("seq", "tp"), P("seq", "tp"))
    return jax.shard_map(body, mesh=mesh, in_specs=in_specs, out_specs=out_specs, check_vma=False)
```

```python
import functools

import jax
import jax.numpy as jnp
from jax import lax
from jax.experimental import pallas as pl
from jax.experimental.pallas import tpu as pltpu
from jax.sharding import PartitionSpec as P

MESH = pl.DeviceIdType.MESH
HEAD_DIM = 128
CLUSTERS = 128
CAP = 256
MOST = 8
EMPTY = 128.0
PAIR = 2 * MOST
STRIDE = 27
PARTS = 4
F32 = jnp.float32
BF16 = jnp.bfloat16


def product(a, b, contract=(1, 0)):
    dims = (((contract[0],), (contract[1],)), ((), ()))
    return lax.dot_general(a, b, dims, preferred_element_type=F32)


def iota(shape, dim):
    return lax.broadcasted_iota(jnp.int32, shape, dim)


def kernel(
    peers,
    ring,
    ids_row,
    normed,
    grad_out,
    wq_hbm,
    wk_hbm,
    wv_hbm,
    wo_hbm,
    result,
    wq,
    wk,
    wv,
    wo,
    packed,
    recv,
    expanded,
    back,
    xin,
    sums_out,
    sums_in,
    before,
    choose,
    gather_rows,
    take,
    count,
    heads,
    total,
    own,
    w_sem,
    go_send,
    go_recv,
    back_send,
    back_recv,
    x_send,
    x_recv,
    r_send,
    r_recv,
):
    s, t = lax.axis_index("seq"), lax.axis_index("tp")
    right, left, across = lax.rem(t + 1, ring), lax.rem(t + ring - 1, ring), lax.rem(t + 2, ring)
    tokens, width = normed.shape
    part_width = width // PARTS
    slots = peers * PAIR
    tile = 256

    weights = [
        pltpu.make_async_copy(src, dst, w_sem.at[i])
        for i, (src, dst) in enumerate(
            ((wq_hbm, wq), (wk_hbm, wk), (wv_hbm, wv), (wo_hbm, wo))
        )
    ]
    for copy in weights:
        copy.start()

    barrier = pltpu.get_barrier_semaphore()

    @pl.loop(1, peers)
    def _(r):
        pl.semaphore_signal(
            barrier, inc=1, device_id=(lax.rem(s + r, peers), t), device_id_type=MESH
        )

    for d in range(1, ring):
        pl.semaphore_signal(
            barrier, inc=1, device_id=(s, lax.rem(t + d, ring)), device_id_type=MESH
        )

    def column(row):
        wide = jnp.broadcast_to(row.astype(F32), (128, tokens))
        blocks = [jnp.transpose(wide[:, i : i + 128]) for i in range(0, tokens, 128)]
        return jnp.concatenate(blocks, axis=0)[:, :1].astype(jnp.int32)

    same = column(ids_row[...]) == ids_row[...]
    above = iota((tokens, tokens), 0) < iota((tokens, tokens), 1)
    rank_row = jnp.sum(jnp.where(same & above, 1.0, 0.0), axis=0, keepdims=True)
    place_row = ((ids_row[...] & 1) * peers + (ids_row[...] >> 1)) * PAIR + rank_row.astype(
        jnp.int32
    )

    def pack(half):
        @pl.loop(0, slots // tile)
        def _(i):
            row = iota((tile, tokens), 0) + (half * slots + i * tile)
            put = (row == place_row).astype(F32)
            put_grad = (row == place_row + MOST).astype(BF16)
            filled = jnp.sum(put, axis=1, keepdims=True)
            rows = product(put.astype(BF16), normed[...]) + product(put_grad, grad_out[...])
            odd = lax.rem(iota((tile, 128), 0), PAIR)
            mark = (odd < MOST) & (filled < 0.5)
            first = jnp.where(mark, EMPTY, rows[:, :128])
            rows = jnp.concatenate([first, rows[:, 128:]], axis=1).astype(BF16)
            for part in range(PARTS):
                some = rows[:, part * part_width : (part + 1) * part_width]
                packed[half, part, pl.ds(i * (tile // PAIR), tile // PAIR)] = some.reshape(
                    tile // PAIR, PAIR, part_width
                )

    def send_all(half, part, src, dst, send_sem, recv_sem):
        pltpu.make_async_copy(
            src.at[half, part, s], dst.at[half, part, s], recv_sem.at[half, part]
        ).start()

        @pl.loop(1, peers)
        def _(r):
            peer = lax.rem(s + r * STRIDE, peers)
            pltpu.make_async_remote_copy(
                src_ref=src.at[half, part, peer],
                dst_ref=dst.at[half, part, s],
                send_sem=send_sem.at[half, part],
                recv_sem=recv_sem.at[half, part],
                device_id=(peer, t),
                device_id_type=MESH,
            ).start()

    def wait_all(half, part, dst, recv_sem):
        everything = dst.at[half, part]
        pltpu.make_async_copy(everything, everything, recv_sem.at[half, part]).wait()

    def wait_sent(half, part, src, send_sem):
        others = src.at[half, part, pl.ds(0, peers - 1)]
        pltpu.make_async_copy(others, others, send_sem.at[half, part]).wait()

    def hop(src, dst, send_sem, recv_sem, target):
        return pltpu.make_async_remote_copy(
            src_ref=src,
            dst_ref=dst,
            send_sem=send_sem,
            recv_sem=recv_sem,
            device_id=(s, target),
            device_id_type=MESH,
        )

    def gather_hop(half, part, i):
        block = xin.at[half, part]
        src, dst, target = (
            (block.at[0, 0], block.at[1, 0], right),
            (block.at[0, 1], block.at[2, 1], left),
            (block.at[0, 1], block.at[1, 1], right),
            (block.at[0, 0], block.at[2, 0], left),
            (block.at[1, 0], block.at[3, 0], right),
            (block.at[2, 1], block.at[3, 1], left),
        )[i]
        return hop(src, dst, x_send.at[half, part, i], x_recv.at[half, part, i], target)

    def sum_hop(half, part, i):
        target = (right, left)[i % 2]
        return hop(
            sums_out.at[half, part, i],
            sums_in.at[half, part, i],
            r_send.at[half, part, i],
            r_recv.at[half, part, i],
            target,
        )

    def rank_slots(half):
        first = recv[half, 0, :, :, :128].astype(F32)
        valid = (first[:, :MOST] < 0.5 * EMPTY).astype(F32)
        zero = jnp.zeros_like(valid)
        only = jnp.concatenate([valid, zero], axis=1).reshape(slots, 128)
        valid = jnp.concatenate([valid, valid], axis=1).reshape(slots, 128)
        rank = product(before[...], only.astype(BF16))
        count[half] = jnp.broadcast_to(jnp.sum(only, axis=0, keepdims=True), (8, 128))
        second = lax.rem(iota((slots, 128), 0), PAIR) >= MOST
        kept = (valid > 0.5) & (rank < CAP)
        goal = jnp.where(kept, rank + jnp.where(second, CAP * 1.0, 0.0), -1.0)
        blocks = [jnp.transpose(goal[i : i + 128]) for i in range(0, slots, 128)]
        goal_row = jnp.concatenate(blocks, axis=1)[:1].astype(jnp.int32)
        goal = goal.astype(jnp.int32)
        for k in range(0, 2 * CAP, 128):
            choose[half, :, k : k + 128] = (goal == iota((slots, 128), 1) + k).astype(BF16)
            gather_rows[half, k : k + 128] = (goal_row == iota((128, slots), 0) + k).astype(BF16)

    def compact(half, part):
        wait_all(half, part, recv, go_recv)
        if part == 0:
            rank_slots(half)
        rows = recv[half, part].reshape(slots, part_width)
        both = product(gather_rows[half], rows).astype(BF16)
        xin[half, part, 0] = both.reshape(2, CAP, part_width)
        for i in range(4):
            gather_hop(half, part, i).start()

    def relay(half, part):
        for i in range(2):
            gather_hop(half, part, i).wait_recv()
            gather_hop(half, part, 4 + i).start()

    def project(half, part):
        for i in range(2, 6):
            gather_hop(half, part, i).wait_recv()
        starts = [
            pl.multiple_of(owner * width + part * part_width, part_width)
            for owner in (t, left, right, across)
        ]

        def add(i, value):
            if part > 0:
                value = total[i] + value
            if part < PARTS - 1:
                total[i] = value
            else:
                heads[i] = value.astype(BF16)

        for i, w in enumerate((wq, wk, wv)):
            value = None
            for k in range(4):
                more = product(xin[half, part, k, 0], w[pl.ds(starts[k], part_width), :])
                value = more if value is None else value + more
            add(i, value)
        value = None
        for k in range(4):
            more = product(xin[half, part, k, 1], wo[:, pl.ds(starts[k], part_width)], (1, 1))
            value = more if value is None else value + more
        add(3, value)

    def attend(half):
        scale = HEAD_DIM ** (-0.5)
        usable = count[half, :1, :1] > iota((1, CAP), 1).astype(F32)

        @pl.loop(0, width // HEAD_DIM, unroll=4)
        def _(h):
            at = pl.ds(pl.multiple_of(h * HEAD_DIM, HEAD_DIM), HEAD_DIM)
            query, key_rows, value_rows, grad_rows = (heads[i, :, at] for i in range(4))
            scores = product(query, key_rows, (1, 1)) * scale
            scores = jnp.where(usable, scores, -1e30)
            raised = jnp.exp(scores - jnp.max(scores, axis=1, keepdims=True))
            probs = raised / jnp.sum(raised, axis=1, keepdims=True)
            rounded = probs.astype(BF16)
            grad_probs = product(grad_rows, value_rows, (1, 1))
            inner = jnp.sum(grad_probs * probs, axis=1, keepdims=True)
            grad_scores = (probs * (grad_probs - inner) * scale).astype(BF16)
            heads[4, :, at] = product(rounded, value_rows).astype(BF16)
            heads[5, :, at] = product(grad_scores, key_rows).astype(BF16)
            heads[6, :, at] = product(grad_scores, query, (0, 0)).astype(BF16)
            heads[7, :, at] = product(rounded, grad_rows, (0, 0)).astype(BF16)

    def out_part(target, part):
        start = pl.multiple_of(target * width + part * part_width, part_width)
        return product(heads[4], wo[:, pl.ds(start, part_width)])

    def grad_part(target, part):
        start = pl.multiple_of(target * width + part * part_width, part_width)
        rows = pl.ds(start, part_width)
        return (
            product(heads[5], wq[rows, :], (1, 1))
            + product(heads[6], wk[rows, :], (1, 1))
            + product(heads[7], wv[rows, :], (1, 1))
        )

    def outputs(half, part):
        for i, target, make in (
            (0, across, out_part),
            (1, across, grad_part),
            (4, right, grad_part),
            (5, left, out_part),
        ):
            sums_out[half, part, i] = make(target, part).astype(BF16)
            sum_hop(half, part, i).start()
        for i, target, make in ((2, right, out_part), (3, left, grad_part)):
            own[half, part, i] = make(target, part)
        own[half, part, 0] = out_part(t, part)
        own[half, part, 1] = grad_part(t, part)

    def combine(half, part):
        for i in (2, 3):
            sum_hop(half, part, i - 2).wait_recv()
            more = sums_in[half, part, i - 2].astype(F32)
            sums_out[half, part, i] = (own[half, part, i] + more).astype(BF16)
            sum_hop(half, part, i).start()

    def finish(half, part):
        for i in range(2, 6):
            sum_hop(half, part, i).wait_recv()
        out, grad = own[half, part, 0], own[half, part, 1]
        for i in range(2, 6):
            more = sums_in[half, part, i].astype(F32)
            if i in (2, 5):
                out = out + more
            else:
                grad = grad + more
        both = jnp.concatenate([out.astype(BF16), grad.astype(BF16)], axis=0)

        @pl.loop(0, slots // tile)
        def _(i):
            rows = product(choose[half, pl.ds(i * tile, tile), :], both).astype(BF16)
            expanded[half, part, pl.ds(i * (tile // PAIR), tile // PAIR)] = rows.reshape(
                tile // PAIR, PAIR, part_width
            )

        send_all(half, part, expanded, back, back_send, back_recv)

    def unpack(half, part):
        wait_all(half, part, back, back_recv)
        rows = back[half, part].reshape(slots, part_width)
        at = pl.ds(part * part_width, part_width)
        out = product(take[half, 0], rows)
        grad = product(take[half, 1], rows)
        for i, value in enumerate((out, grad)):
            if half == 1:
                value = result[i, :, at].astype(F32) + value
            result[i, :, at] = value.astype(BF16)

    everything = [(half, part) for half in range(2) for part in range(PARTS)]
    pack(0)
    pl.semaphore_wait(barrier, peers - 1 + ring - 1)
    for part in range(PARTS):
        send_all(0, part, packed, recv, go_send, go_recv)
    pack(1)
    for part in range(PARTS):
        send_all(1, part, packed, recv, go_send, go_recv)

    @pl.loop(0, slots // tile)
    def _(i):
        row, other_row = iota((tile, slots), 0) + i * tile, iota((tile, slots), 1)
        number = (row >> 4) * MOST + (row & (MOST - 1))
        other = (other_row >> 4) * MOST + (other_row & (MOST - 1))
        before[pl.ds(i * tile, tile), :] = (other < number).astype(BF16)

    place_column = column(place_row)
    for half in range(2):
        lane = iota((tokens, slots), 1) + half * slots
        take[half, 0] = (lane == place_column).astype(BF16)
        take[half, 1] = (lane == place_column + MOST).astype(BF16)

    for copy in weights:
        copy.wait()

    compact(0, 0)
    relay(0, 0)
    compact(0, 1)
    relay(0, 1)
    compact(0, 2)
    compact(0, 3)
    relay(0, 2)
    relay(0, 3)
    compact(1, 0)
    project(0, 0)
    project(0, 1)
    project(0, 2)
    relay(1, 0)
    project(0, 3)
    compact(1, 1)
    attend(0)
    outputs(0, 0)
    outputs(0, 1)
    outputs(0, 2)
    outputs(0, 3)
    combine(0, 0)
    compact(1, 2)
    combine(0, 1)
    combine(0, 2)
    combine(0, 3)
    compact(1, 3)
    relay(1, 1)
    relay(1, 2)
    finish(0, 0)
    finish(0, 1)
    finish(0, 2)
    relay(1, 3)
    finish(0, 3)
    project(1, 0)
    project(1, 1)
    project(1, 2)
    project(1, 3)
    attend(1)
    outputs(1, 0)
    combine(1, 0)
    outputs(1, 1)
    outputs(1, 2)
    finish(1, 0)
    combine(1, 1)
    combine(1, 2)
    outputs(1, 3)
    finish(1, 1)
    finish(1, 2)
    unpack(0, 0)
    unpack(0, 1)
    unpack(0, 2)
    unpack(0, 3)
    combine(1, 3)
    finish(1, 3)
    unpack(1, 0)
    unpack(1, 1)
    unpack(1, 2)
    unpack(1, 3)

    for half, part in everything:
        wait_sent(half, part, packed, go_send)
        wait_sent(half, part, expanded, back_send)
        for i in range(6):
            gather_hop(half, part, i).wait_send()
            sum_hop(half, part, i).wait_send()


def body(normed, cluster, w_query, w_key, w_value, w_out, grad_out):
    peers, ring = lax.axis_size("seq"), lax.axis_size("tp")
    tokens, width = normed.shape
    slots = peers * PAIR
    part_width = width // PARTS
    vmem = pl.BlockSpec(memory_space=pltpu.VMEM)
    anywhere = pl.BlockSpec(memory_space=pl.ANY)
    dma = pltpu.SemaphoreType.DMA
    result = pl.pallas_call(
        functools.partial(kernel, peers, ring),
        out_shape=jax.ShapeDtypeStruct((2, tokens, width), BF16),
        in_specs=[vmem] * 3 + [anywhere] * 4,
        out_specs=vmem,
        scratch_shapes=[
            pltpu.VMEM(w_query.shape, BF16),
            pltpu.VMEM(w_key.shape, BF16),
            pltpu.VMEM(w_value.shape, BF16),
            pltpu.VMEM(w_out.shape, BF16),
            pltpu.VMEM((2, PARTS, peers, PAIR, part_width), BF16),
            pltpu.VMEM((2, PARTS, peers, PAIR, part_width), BF16),
            pltpu.VMEM((2, PARTS, peers, PAIR, part_width), BF16),
            pltpu.VMEM((2, PARTS, peers, PAIR, part_width), BF16),
            pltpu.VMEM((2, PARTS, ring, 2, CAP, part_width), BF16),
            pltpu.VMEM((2, PARTS, 6, CAP, part_width), BF16),
            pltpu.VMEM((2, PARTS, 6, CAP, part_width), BF16),
            pltpu.VMEM((slots, slots), BF16),
            pltpu.VMEM((2, slots, 2 * CAP), BF16),
            pltpu.VMEM((2, 2 * CAP, slots), BF16),
            pltpu.VMEM((2, 2, tokens, slots), BF16),
            pltpu.VMEM((2, 8, 128), F32),
            pltpu.VMEM((8, CAP, width), BF16),
            pltpu.VMEM((4, CAP, width), F32),
            pltpu.VMEM((2, PARTS, 4, CAP, part_width), F32),
            dma((4,)),
            dma((2, PARTS)),
            dma((2, PARTS)),
            dma((2, PARTS)),
            dma((2, PARTS)),
            dma((2, PARTS, 6)),
            dma((2, PARTS, 6)),
            dma((2, PARTS, 6)),
            dma((2, PARTS, 6)),
        ],
        compiler_params=pltpu.CompilerParams(
            collective_id=0, has_side_effects=True, vmem_limit_bytes=60 * 2**20
        ),
        name="routed",
    )(cluster.reshape(1, tokens), normed, grad_out, w_query, w_key, w_value, w_out)
    return (result[0], result[1].astype(F32))


def solution(mesh):
    in_specs = (
        P("seq", "tp"),
        P("seq", None),
        P(None, "tp"),
        P(None, "tp"),
        P(None, "tp"),
        P("tp", None),
        P("seq", "tp"),
    )
    out_specs = (P("seq", "tp"), P("seq", "tp"))
    return jax.shard_map(body, mesh=mesh, in_specs=in_specs, out_specs=out_specs, check_vma=False)
```

```python
import functools

import jax
import jax.numpy as jnp
from jax import lax
from jax.experimental import pallas as pl
from jax.experimental.pallas import tpu as pltpu
from jax.sharding import PartitionSpec as P

MESH = pl.DeviceIdType.MESH
HEAD_DIM = 128
CLUSTERS = 128
CAP = 256
MOST = 8
EMPTY = 128.0
PAIR = 2 * MOST
STRIDE = 27
PARTS = 4
F32 = jnp.float32
BF16 = jnp.bfloat16


def product(a, b, contract=(1, 0)):
    dims = (((contract[0],), (contract[1],)), ((), ()))
    return lax.dot_general(a, b, dims, preferred_element_type=F32)


def iota(shape, dim):
    return lax.broadcasted_iota(jnp.int32, shape, dim)


def kernel(
    peers,
    ring,
    ids_row,
    normed,
    grad_out,
    wq_hbm,
    wk_hbm,
    wv_hbm,
    wo_hbm,
    result,
    wq,
    wk,
    wv,
    wo,
    packed,
    recv,
    expanded,
    back,
    xin,
    sums_out,
    sums_in,
    before,
    choose,
    gather_rows,
    take,
    count,
    heads,
    total,
    own,
    w_sem,
    go_send,
    go_recv,
    back_send,
    back_recv,
    x_send,
    x_recv,
    r_send,
    r_recv,
):
    s, t = lax.axis_index("seq"), lax.axis_index("tp")
    right, left, across = lax.rem(t + 1, ring), lax.rem(t + ring - 1, ring), lax.rem(t + 2, ring)
    tokens, width = normed.shape
    part_width = width // PARTS
    slots = peers * PAIR
    tile = 256

    weights = [
        pltpu.make_async_copy(src, dst, w_sem.at[i])
        for i, (src, dst) in enumerate(
            ((wq_hbm, wq), (wk_hbm, wk), (wv_hbm, wv), (wo_hbm, wo))
        )
    ]
    for copy in weights:
        copy.start()

    barrier = pltpu.get_barrier_semaphore()

    @pl.loop(1, peers)
    def _(r):
        pl.semaphore_signal(
            barrier, inc=1, device_id=(lax.rem(s + r, peers), t), device_id_type=MESH
        )

    for d in range(1, ring):
        pl.semaphore_signal(
            barrier, inc=1, device_id=(s, lax.rem(t + d, ring)), device_id_type=MESH
        )

    def column(row):
        wide = jnp.broadcast_to(row.astype(F32), (128, tokens))
        blocks = [jnp.transpose(wide[:, i : i + 128]) for i in range(0, tokens, 128)]
        return jnp.concatenate(blocks, axis=0)[:, :1].astype(jnp.int32)

    same = column(ids_row[...]) == ids_row[...]
    above = iota((tokens, tokens), 0) < iota((tokens, tokens), 1)
    rank_row = jnp.sum(jnp.where(same & above, 1.0, 0.0), axis=0, keepdims=True)
    place_row = ((ids_row[...] & 1) * peers + (ids_row[...] >> 1)) * PAIR + rank_row.astype(
        jnp.int32
    )

    def pack(half):
        @pl.loop(0, slots // tile)
        def _(i):
            row = iota((tile, tokens), 0) + (half * slots + i * tile)
            put = (row == place_row).astype(F32)
            put_grad = (row == place_row + MOST).astype(BF16)
            filled = jnp.sum(put, axis=1, keepdims=True)
            rows = product(put.astype(BF16), normed[...]) + product(put_grad, grad_out[...])
            odd = lax.rem(iota((tile, 128), 0), PAIR)
            mark = (odd < MOST) & (filled < 0.5)
            first = jnp.where(mark, EMPTY, rows[:, :128])
            rows = jnp.concatenate([first, rows[:, 128:]], axis=1).astype(BF16)
            for part in range(PARTS):
                some = rows[:, part * part_width : (part + 1) * part_width]
                packed[half, part, pl.ds(i * (tile // PAIR), tile // PAIR)] = some.reshape(
                    tile // PAIR, PAIR, part_width
                )

    def send_all(half, part, src, dst, send_sem, recv_sem):
        pltpu.make_async_copy(
            src.at[half, part, s], dst.at[half, part, s], recv_sem.at[half, part]
        ).start()

        @pl.loop(1, peers, unroll=7)
        def _(r):
            peer = lax.rem(s + r * STRIDE, peers)
            pltpu.make_async_remote_copy(
                src_ref=src.at[half, part, peer],
                dst_ref=dst.at[half, part, s],
                send_sem=send_sem.at[half, part],
                recv_sem=recv_sem.at[half, part],
                device_id=(peer, t),
                device_id_type=MESH,
            ).start()

    def wait_all(half, part, dst, recv_sem):
        everything = dst.at[half, part]
        pltpu.make_async_copy(everything, everything, recv_sem.at[half, part]).wait()

    def wait_sent(half, part, src, send_sem):
        others = src.at[half, part, pl.ds(0, peers - 1)]
        pltpu.make_async_copy(others, others, send_sem.at[half, part]).wait()

    def hop(src, dst, send_sem, recv_sem, target):
        return pltpu.make_async_remote_copy(
            src_ref=src,
            dst_ref=dst,
            send_sem=send_sem,
            recv_sem=recv_sem,
            device_id=(s, target),
            device_id_type=MESH,
        )

    def gather_hop(half, part, i):
        block = xin.at[half, part]
        src, dst, target = (
            (block.at[0, 0], block.at[1, 0], right),
            (block.at[0, 1], block.at[2, 1], left),
            (block.at[0, 1], block.at[1, 1], right),
            (block.at[0, 0], block.at[2, 0], left),
            (block.at[1, 0], block.at[3, 0], right),
            (block.at[2, 1], block.at[3, 1], left),
        )[i]
        return hop(src, dst, x_send.at[half, part, i], x_recv.at[half, part, i], target)

    def sum_hop(half, part, i):
        target = (right, left)[i % 2]
        return hop(
            sums_out.at[half, part, i],
            sums_in.at[half, part, i],
            r_send.at[half, part, i],
            r_recv.at[half, part, i],
            target,
        )

    def rank_slots(half):
        first = recv[half, 0, :, :, :128].astype(F32)
        valid = (first[:, :MOST] < 0.5 * EMPTY).astype(F32)
        zero = jnp.zeros_like(valid)
        only = jnp.concatenate([valid, zero], axis=1).reshape(slots, 128)
        valid = jnp.concatenate([valid, valid], axis=1).reshape(slots, 128)
        rank = product(before[...], only.astype(BF16))
        count[half] = jnp.broadcast_to(jnp.sum(only, axis=0, keepdims=True), (8, 128))
        second = lax.rem(iota((slots, 128), 0), PAIR) >= MOST
        kept = (valid > 0.5) & (rank < CAP)
        goal = jnp.where(kept, rank + jnp.where(second, CAP * 1.0, 0.0), -1.0)
        blocks = [jnp.transpose(goal[i : i + 128]) for i in range(0, slots, 128)]
        goal_row = jnp.concatenate(blocks, axis=1)[:1].astype(jnp.int32)
        goal = goal.astype(jnp.int32)
        for k in range(0, 2 * CAP, 128):
            choose[half, :, k : k + 128] = (goal == iota((slots, 128), 1) + k).astype(BF16)
            gather_rows[half, k : k + 128] = (goal_row == iota((128, slots), 0) + k).astype(BF16)

    def compact(half, part):
        wait_all(half, part, recv, go_recv)
        if part == 0:
            rank_slots(half)
        rows = recv[half, part].reshape(slots, part_width)
        both = product(gather_rows[half], rows).astype(BF16)
        xin[half, part, 0] = both.reshape(2, CAP, part_width)
        for i in range(4):
            gather_hop(half, part, i).start()

    def relay(half, part):
        for i in range(2):
            gather_hop(half, part, i).wait_recv()
            gather_hop(half, part, 4 + i).start()

    def project(half, part):
        for i in range(2, 6):
            gather_hop(half, part, i).wait_recv()
        starts = [
            pl.multiple_of(owner * width + part * part_width, part_width)
            for owner in (t, left, right, across)
        ]

        def add(i, value):
            if part > 0:
                value = total[i] + value
            if part < PARTS - 1:
                total[i] = value
            else:
                heads[i] = value.astype(BF16)

        for i, w in enumerate((wq, wk, wv)):
            value = None
            for k in range(4):
                more = product(xin[half, part, k, 0], w[pl.ds(starts[k], part_width), :])
                value = more if value is None else value + more
            add(i, value)
        value = None
        for k in range(4):
            more = product(xin[half, part, k, 1], wo[:, pl.ds(starts[k], part_width)], (1, 1))
            value = more if value is None else value + more
        add(3, value)

    def attend(half):
        scale = HEAD_DIM ** (-0.5)
        usable = count[half, :1, :1] > iota((1, CAP), 1).astype(F32)

        @pl.loop(0, width // HEAD_DIM, unroll=4)
        def _(h):
            at = pl.ds(pl.multiple_of(h * HEAD_DIM, HEAD_DIM), HEAD_DIM)
            query, key_rows, value_rows, grad_rows = (heads[i, :, at] for i in range(4))
            scores = product(query, key_rows, (1, 1)) * scale
            scores = jnp.where(usable, scores, -1e30)
            raised = jnp.exp(scores - jnp.max(scores, axis=1, keepdims=True))
            probs = raised / jnp.sum(raised, axis=1, keepdims=True)
            rounded = probs.astype(BF16)
            grad_probs = product(grad_rows, value_rows, (1, 1))
            inner = jnp.sum(grad_probs * probs, axis=1, keepdims=True)
            grad_scores = (probs * (grad_probs - inner) * scale).astype(BF16)
            heads[4, :, at] = product(rounded, value_rows).astype(BF16)
            heads[5, :, at] = product(grad_scores, key_rows).astype(BF16)
            heads[6, :, at] = product(grad_scores, query, (0, 0)).astype(BF16)
            heads[7, :, at] = product(rounded, grad_rows, (0, 0)).astype(BF16)

    def out_part(target, part):
        start = pl.multiple_of(target * width + part * part_width, part_width)
        return product(heads[4], wo[:, pl.ds(start, part_width)])

    def grad_part(target, part):
        start = pl.multiple_of(target * width + part * part_width, part_width)
        rows = pl.ds(start, part_width)
        return (
            product(heads[5], wq[rows, :], (1, 1))
            + product(heads[6], wk[rows, :], (1, 1))
            + product(heads[7], wv[rows, :], (1, 1))
        )

    def outputs(half, part):
        for i, target, make in (
            (0, across, out_part),
            (1, across, grad_part),
            (4, right, grad_part),
            (5, left, out_part),
        ):
            sums_out[half, part, i] = make(target, part).astype(BF16)
            sum_hop(half, part, i).start()
        for i, target, make in ((2, right, out_part), (3, left, grad_part)):
            own[half, part, i] = make(target, part)
        own[half, part, 0] = out_part(t, part)
        own[half, part, 1] = grad_part(t, part)

    def combine(half, part):
        for i in (2, 3):
            sum_hop(half, part, i - 2).wait_recv()
            more = sums_in[half, part, i - 2].astype(F32)
            sums_out[half, part, i] = (own[half, part, i] + more).astype(BF16)
            sum_hop(half, part, i).start()

    def finish(half, part):
        for i in range(2, 6):
            sum_hop(half, part, i).wait_recv()
        out, grad = own[half, part, 0], own[half, part, 1]
        for i in range(2, 6):
            more = sums_in[half, part, i].astype(F32)
            if i in (2, 5):
                out = out + more
            else:
                grad = grad + more
        both = jnp.concatenate([out.astype(BF16), grad.astype(BF16)], axis=0)

        @pl.loop(0, slots // tile)
        def _(i):
            rows = product(choose[half, pl.ds(i * tile, tile), :], both).astype(BF16)
            expanded[half, part, pl.ds(i * (tile // PAIR), tile // PAIR)] = rows.reshape(
                tile // PAIR, PAIR, part_width
            )

        send_all(half, part, expanded, back, back_send, back_recv)

    def unpack(half, part):
        wait_all(half, part, back, back_recv)
        rows = back[half, part].reshape(slots, part_width)
        at = pl.ds(part * part_width, part_width)
        out = product(take[half, 0], rows)
        grad = product(take[half, 1], rows)
        for i, value in enumerate((out, grad)):
            if half == 1:
                value = result[i, :, at].astype(F32) + value
            result[i, :, at] = value.astype(BF16)

    everything = [(half, part) for half in range(2) for part in range(PARTS)]
    pack(0)
    pl.semaphore_wait(barrier, peers - 1 + ring - 1)
    for part in range(PARTS):
        send_all(0, part, packed, recv, go_send, go_recv)
    pack(1)
    for part in range(PARTS):
        send_all(1, part, packed, recv, go_send, go_recv)

    @pl.loop(0, slots // tile)
    def _(i):
        row, other_row = iota((tile, slots), 0) + i * tile, iota((tile, slots), 1)
        number = (row >> 4) * MOST + (row & (MOST - 1))
        other = (other_row >> 4) * MOST + (other_row & (MOST - 1))
        before[pl.ds(i * tile, tile), :] = (other < number).astype(BF16)

    place_column = column(place_row)
    for half in range(2):
        lane = iota((tokens, slots), 1) + half * slots
        take[half, 0] = (lane == place_column).astype(BF16)
        take[half, 1] = (lane == place_column + MOST).astype(BF16)

    for copy in weights:
        copy.wait()

    compact(0, 0)
    relay(0, 0)
    compact(0, 1)
    relay(0, 1)
    compact(0, 2)
    compact(0, 3)
    relay(0, 2)
    relay(0, 3)
    compact(1, 0)
    project(0, 0)
    project(0, 1)
    project(0, 2)
    relay(1, 0)
    project(0, 3)
    compact(1, 1)
    attend(0)
    outputs(0, 0)
    outputs(0, 1)
    outputs(0, 2)
    outputs(0, 3)
    combine(0, 0)
    compact(1, 2)
    combine(0, 1)
    combine(0, 2)
    combine(0, 3)
    compact(1, 3)
    relay(1, 1)
    relay(1, 2)
    finish(0, 0)
    finish(0, 1)
    finish(0, 2)
    relay(1, 3)
    finish(0, 3)
    project(1, 0)
    project(1, 1)
    project(1, 2)
    project(1, 3)
    attend(1)
    outputs(1, 0)
    combine(1, 0)
    outputs(1, 1)
    outputs(1, 2)
    finish(1, 0)
    combine(1, 1)
    combine(1, 2)
    outputs(1, 3)
    finish(1, 1)
    finish(1, 2)
    unpack(0, 0)
    unpack(0, 1)
    unpack(0, 2)
    unpack(0, 3)
    combine(1, 3)
    finish(1, 3)
    unpack(1, 0)
    unpack(1, 1)
    unpack(1, 2)
    unpack(1, 3)

    for half, part in everything:
        wait_sent(half, part, packed, go_send)
        wait_sent(half, part, expanded, back_send)
        for i in range(6):
            gather_hop(half, part, i).wait_send()
            sum_hop(half, part, i).wait_send()


def body(normed, cluster, w_query, w_key, w_value, w_out, grad_out):
    peers, ring = lax.axis_size("seq"), lax.axis_size("tp")
    tokens, width = normed.shape
    slots = peers * PAIR
    part_width = width // PARTS
    vmem = pl.BlockSpec(memory_space=pltpu.VMEM)
    anywhere = pl.BlockSpec(memory_space=pl.ANY)
    dma = pltpu.SemaphoreType.DMA
    result = pl.pallas_call(
        functools.partial(kernel, peers, ring),
        out_shape=jax.ShapeDtypeStruct((2, tokens, width), BF16),
        in_specs=[vmem] * 3 + [anywhere] * 4,
        out_specs=vmem,
        scratch_shapes=[
            pltpu.VMEM(w_query.shape, BF16),
            pltpu.VMEM(w_key.shape, BF16),
            pltpu.VMEM(w_value.shape, BF16),
            pltpu.VMEM(w_out.shape, BF16),
            pltpu.VMEM((2, PARTS, peers, PAIR, part_width), BF16),
            pltpu.VMEM((2, PARTS, peers, PAIR, part_width), BF16),
            pltpu.VMEM((2, PARTS, peers, PAIR, part_width), BF16),
            pltpu.VMEM((2, PARTS, peers, PAIR, part_width), BF16),
            pltpu.VMEM((2, PARTS, ring, 2, CAP, part_width), BF16),
            pltpu.VMEM((2, PARTS, 6, CAP, part_width), BF16),
            pltpu.VMEM((2, PARTS, 6, CAP, part_width), BF16),
            pltpu.VMEM((slots, slots), BF16),
            pltpu.VMEM((2, slots, 2 * CAP), BF16),
            pltpu.VMEM((2, 2 * CAP, slots), BF16),
            pltpu.VMEM((2, 2, tokens, slots), BF16),
            pltpu.VMEM((2, 8, 128), F32),
            pltpu.VMEM((8, CAP, width), BF16),
            pltpu.VMEM((4, CAP, width), F32),
            pltpu.VMEM((2, PARTS, 4, CAP, part_width), F32),
            dma((4,)),
            dma((2, PARTS)),
            dma((2, PARTS)),
            dma((2, PARTS)),
            dma((2, PARTS)),
            dma((2, PARTS, 6)),
            dma((2, PARTS, 6)),
            dma((2, PARTS, 6)),
            dma((2, PARTS, 6)),
        ],
        compiler_params=pltpu.CompilerParams(
            collective_id=0, has_side_effects=True, vmem_limit_bytes=60 * 2**20
        ),
        name="routed",
    )(cluster.reshape(1, tokens), normed, grad_out, w_query, w_key, w_value, w_out)
    return (result[0], result[1].astype(F32))


def solution(mesh):
    in_specs = (
        P("seq", "tp"),
        P("seq", None),
        P(None, "tp"),
        P(None, "tp"),
        P(None, "tp"),
        P("tp", None),
        P("seq", "tp"),
    )
    out_specs = (P("seq", "tp"), P("seq", "tp"))
    return jax.shard_map(body, mesh=mesh, in_specs=in_specs, out_specs=out_specs, check_vma=False)
```
